768 devices in a mesh: fsdp: 24 (over z_hi, x, core), ctx: 32 (over z_lo, y).
Axes of the slice: x: 4, y: 8, z: 12 (z_hi: 3, z_lo: 4; z = z_hi * 4 + z_lo), core: 2. Of those that a mesh axis runs over, the one named last changes fastest.
Arguments:
- frames: bfloat16 [24, 16384, 1536], P('fsdp', 'ctx'), may hold values from -120 to 120
- lengths: int32 [24], P('fsdp'), may hold values from 4096 to 16384, as said below
- ln_gain: float32 [1536], replicated, may hold values from 0.1 to 1.9
- w_in: bfloat16 [1536, 1536], P('fsdp'), may hold values from -0.15625 to 0.15625
- dw_kernel: float32 [31, 768], replicated, may hold values from -1 to 1
- bn_gain: float32 [768], replicated, may hold values from 0.1 to 1.9
- bn_shift: float32 [768], replicated, may hold values from -3 to 3
- w_out: bfloat16 [768, 1536], P('fsdp'), may hold values from -0.21875 to 0.21875
Outputs:
- result: bfloat16 [24, 16384, 1536], P('fsdp', 'ctx')
The draws below stay inside these ranges and needn't reach their ends.
Inputs may be any that keep to these rules, and one draw needn't show every extreme that they name: frames 0 to lengths[r] - 1 of recording r are valid; one recording is full and one has exactly 4096 valid frames.
All inputs are finite; a program needn't handle non-finite values.
Results may differ from the reference program's by a relative error of at most 0.0076.
Values may be sent and summed in bfloat16 or wider, within the bound.
A program may use at most 32 MiB of HBM per device.

```python
import math
import jax
import jax.numpy as jnp
from jax import lax

D = 1536
CH = 768
KERNEL = 31
HALF = 15
ROWS = 512
FRAMES = 16384
RECS = 24


def draw_lengths(key, part):
    first_key, second_key = jax.random.split(jax.random.fold_in(key, 11))
    drawn = jax.random.randint(first_key, (RECS,), FRAMES // 4, FRAMES + 1, dtype=jnp.int32)
    order = jax.random.permutation(second_key, RECS)
    drawn = jnp.where(order == 0, FRAMES, drawn)
    drawn = jnp.where(order == 1, FRAMES // 4, drawn)
    return drawn.astype(jnp.int32)


def draw_frames(key, part):
    noise_key, start_key, drift_key, scale_key = jax.random.split(jax.random.fold_in(key, 23), 4)
    lag_count = 12
    weights = [math.exp(-lag / 4.0) for lag in range(lag_count)]
    weight_norm = math.sqrt(sum((value * value for value in weights)))
    ramp = (jnp.arange(FRAMES, dtype=jnp.float32) / FRAMES)[None, :, None]
    block_count = FRAMES // ROWS
    white = jax.random.normal(noise_key, (RECS, FRAMES + lag_count - 1, D), jnp.float32)
    row_scale = 1.0
    level = 1.5
    noise = jnp.zeros((RECS, FRAMES, D), jnp.float32)
    for lag in range(lag_count):
        noise = noise + white[:, lag:lag + FRAMES] * (weights[lag] / weight_norm)
    block_start = jax.random.normal(start_key, (RECS, block_count, 1, D), jnp.float32) * level
    start = jnp.broadcast_to(block_start, (RECS, block_count, ROWS, D)).reshape(RECS, FRAMES, D)
    drift = jax.random.normal(drift_key, (RECS, 1, D), jnp.float32) * 0.7
    return jnp.clip((noise + start + drift * ramp) * row_scale, -120.0, 120.0).astype(jnp.bfloat16)


def levels(key, shape, shards, low, high):
    factor_of, own = 1.0, jax.random.fold_in(key, 6)
    for axis_at, parts in shards:
        steps = jnp.exp(jax.random.uniform(jax.random.fold_in(own, axis_at), (parts,), jnp.float32, low / len(shards), high / len(shards)))
        factor_of = factor_of * jnp.repeat(steps, shape[axis_at] // parts).reshape([-1 if axis == axis_at else 1 for axis in range(len(shape))])
    return factor_of


def scatter_about(rng, shape, deviation, bound, pieces=(), kind=jnp.bfloat16):
    entries = jax.random.normal(rng, shape, jnp.float32) * deviation
    if len(pieces) > 0:
        entries = levels(rng, shape, pieces, -0.22, 0.18) * entries
    return jnp.clip(entries, min=-bound, max=bound).astype(kind)


def setup_inputs(seed: int = 0) -> dict:
    keys = jax.random.split(jax.random.key(seed), 9)
    frames = draw_frames(jax.random.fold_in(keys[8], 71), 0)
    lengths = draw_lengths(jax.random.fold_in(keys[8], 71), 0)
    ln_gain = jnp.clip(1.0 + 0.18 * jax.random.normal(keys[2], (D,), jnp.float32), 0.1, 1.9)
    w_in = scatter_about(keys[3], (D, 2 * CH), D ** -0.5, 0.15625, ((0, 24),))
    dw_kernel = scatter_about(keys[4], (KERNEL, CH), KERNEL ** -0.5, 1.0, (), jnp.float32)
    bn_gain = jnp.clip(1.0 + 0.18 * jax.random.normal(keys[5], (CH,), jnp.float32), 0.1, 1.9)
    bn_shift = scatter_about(keys[6], (CH,), 0.5, 3.0, (), jnp.float32)
    w_out = scatter_about(keys[7], (CH, D), CH ** -0.5, 0.21875, ((0, 24),))
    return dict(frames=frames, lengths=lengths, ln_gain=ln_gain, w_in=w_in, dw_kernel=dw_kernel, bn_gain=bn_gain, bn_shift=bn_shift, w_out=w_out)


def normalize_rows(rows_in, ln_gain):
    values = rows_in.astype(jnp.float32)
    centre = lax.optimization_barrier(jnp.mean(values, axis=-1, keepdims=True))
    deviate = values - centre
    spread = lax.optimization_barrier(jnp.mean(deviate * deviate, axis=-1, keepdims=True))
    return (deviate * lax.rsqrt(spread + 1e-05) * ln_gain).astype(jnp.bfloat16)

def reference(frames, lengths, ln_gain, w_in, dw_kernel, bn_gain, bn_shift, w_out):
    position = jnp.arange(FRAMES, dtype=jnp.int32)

    def front_half(record_pair):
        record, length = record_pair
        normed = normalize_rows(record, ln_gain)
        projected = jnp.dot(normed, w_in, preferred_element_type=jnp.float32)
        valid_rows = (position < length)[:, None]
        gated = jnp.where(valid_rows, projected[:, :CH] * jax.nn.sigmoid(projected[:, CH:]), 0.0).astype(jnp.bfloat16)
        padded = jnp.pad(gated.astype(jnp.float32), ((HALF, HALF), (0, 0)))
        convolved = jnp.zeros((FRAMES, CH), jnp.float32)
        for tap_index in range(KERNEL):
            convolved = convolved + padded[tap_index:tap_index + FRAMES] * dw_kernel[tap_index]
        return convolved
    convolved = lax.map(front_half, (frames, lengths.astype(jnp.int32)))
    valid_mask = (position[None, :] < lengths[:, None]).astype(jnp.float32)[:, :, None]
    valid_count = jnp.sum(valid_mask)
    chan_mean = lax.optimization_barrier(jnp.sum(convolved * valid_mask, axis=(0, 1))) / valid_count
    centered = (convolved - chan_mean) * valid_mask
    chan_var = lax.optimization_barrier(jnp.sum(centered * centered, axis=(0, 1))) / valid_count

    def back_half(record_pair):
        conv_block, length = record_pair
        scaled = (conv_block - chan_mean) * lax.rsqrt(chan_var + 1e-05) * bn_gain + bn_shift
        activated = jax.nn.silu(scaled).astype(jnp.bfloat16)
        result_rows = jnp.dot(activated, w_out, preferred_element_type=jnp.float32)
        valid_rows = (position < length)[:, None]
        return jnp.where(valid_rows, result_rows, 0.0).astype(jnp.bfloat16)
    return lax.map(back_half, (convolved, lengths.astype(jnp.int32)))
```

```python
import jax
import jax.numpy as jnp
from jax import lax
from jax.experimental import pallas as pl
from jax.experimental.pallas import tpu as pltpu
from jax.sharding import PartitionSpec as P

MESH = pl.DeviceIdType.MESH
BF16 = jnp.bfloat16
F32 = jnp.float32
NX, NY, NZ = 4, 8, 12
ROWS, EDGE = 512, 16
ALL = ROWS + 2 * EDGE
TAPS, CH, D = 31, 768, 1536
STRIPS = CH // 128
LAYERS = 3
ZS, XS, YS, CS = 0, 2, 11, 17
SEMS = 23


def device_of(x, y, z, c):
    return (((z // 4) * NX + x) * 2 + c, (z % 4) * NY + y)


def sigmoid(v):
    return 0.5 * jnp.tanh(0.5 * v) + 0.5


def combine(all_ref, parts):
    means = [all_ref[i, 0:8, :] for i in range(parts)]
    counts = [all_ref[i, 6:7, :] for i in range(parts)]
    squares = [all_ref[i, 8:16, :] for i in range(parts)]
    total = sum(counts[1:], counts[0])
    inverse = 1.0 / jnp.maximum(total, 1.0)
    weighted = [m * n for m, n in zip(means, counts)]
    mean = sum(weighted[1:], weighted[0]) * inverse
    spread = sum(squares[1:], squares[0])
    for m, n in zip(means, counts):
        spread = spread + n * (m - mean) * (m - mean)
    row = lax.broadcasted_iota(jnp.int32, (8, 128), 0)
    mean = jnp.where(row == 6, jnp.broadcast_to(total, (8, 128)), mean)
    return mean, spread


def kernel(
    frames, lengths, ln_gain, w_in, dw, bn_gain, bn_shift, w_out, out,
    xbuf, nbuf, wbuf, vbuf, acc, gbuf, cbuf, act, r1, r2, r3, final,
    gsend, grecv, hsend, hrecv, ssend, srecv, lsem,
):
    f, t = lax.axis_index("fsdp"), lax.axis_index("ctx")
    x, c = (f // 2) % NX, f % 2
    y = t % NY
    zh, zl = f // (2 * NX), t // NY
    z = zh * 4 + zl
    par = y % 2
    up, down = (zh + 1) % 3, (zh + 2) % 3
    groups = (zh, up, down)

    def at(dx=0, dy=0, dz=0, dc=0):
        return device_of((x + dx) % NX, (y + dy) % NY, (z + dz) % NZ, (c + dc) % 2)

    left, right = (f, (t + 31) % 32), (f, (t + 1) % 32)
    slot1 = x * 2 + c

    def peer1(d):
        to = (slot1 + d) % 8
        return device_of(to // 2, y, z, to % 2)

    peers = [left, right]
    peers += [peer1(d) for d in range(1, 8)]
    peers += [at(dy=d) for d in range(1, NY)]
    peers += [at(dz=d) for d in range(1, NZ)]

    rows_of = [par * 32, par * 32 + 16, par * 16]
    other_of = [(1 - par) * 32, (1 - par) * 32 + 16, (1 - par) * 16]
    bufs = [wbuf, wbuf, vbuf]
    shards = [w_in, w_in, w_out]

    def span(start):
        return pl.ds(pl.multiple_of(start, 16), 16)

    own_frames = pltpu.make_async_copy(frames.at[0], xbuf.at[pl.ds(EDGE, ROWS)], lsem.at[0])
    own_frames.start()
    own_rows = []
    for layer in range(LAYERS):
        copy = pltpu.make_async_copy(
            shards[layer].at[span(rows_of[layer])],
            bufs[layer].at[zh, x, c, span(rows_of[layer])],
            lsem.at[1 + layer],
        )
        copy.start()
        own_rows.append(copy)

    barrier = pltpu.get_barrier_semaphore()
    for peer in peers:
        pl.semaphore_signal(barrier, inc=1, device_id=peer, device_id_type=MESH)
    pl.semaphore_wait(barrier, len(peers))

    sent = []

    def remote(src, dst, sems, k, to):
        return pltpu.make_async_remote_copy(
            src_ref=src, dst_ref=dst, send_sem=sems[0].at[k], recv_sem=sems[1].at[k],
            device_id=to, device_id_type=MESH,
        )

    def send(*args):
        copy = remote(*args)
        copy.start()
        sent.append(copy)

    def arrived(dst, sems, k):
        remote(dst, dst, sems, k, at(dc=1)).wait_recv()

    def gs(layer):
        return (gsend.at[layer], grecv.at[layer])

    XD = (1, 3, 2)

    def unit(layer, group, xs):
        return bufs[layer].at[group, xs, c, span(rows_of[layer])]

    def z_send(layer):
        src = shards[layer].at[span(rows_of[layer])]
        dst = unit(layer, zh, x)
        send(src, dst, gs(layer), ZS + 0, at(dz=-4))
        send(src, dst, gs(layer), ZS + 1, at(dz=4))

    def z_wait(layer):
        arrived(unit(layer, up, x), gs(layer), ZS + 0)
        arrived(unit(layer, down, x), gs(layer), ZS + 1)

    def x_send(layer, which):
        dst = unit(layer, groups[which], x)
        src = shards[layer].at[span(rows_of[layer])] if which == 0 else dst
        for i, d in enumerate(XD):
            send(src, dst, gs(layer), XS + which * 3 + i, at(dx=d))

    def x_wait(layer, which):
        for i, d in enumerate(XD):
            arrived(unit(layer, groups[which], (x + 4 - d) % NX), gs(layer), XS + which * 3 + i)

    def piece(layer, group, rows, side):
        return bufs[layer].at[group, :, c, span(rows), pl.ds(side * CH, CH)]

    def y_send(layer, which):
        for side, d in ((0, 1), (1, 7)):
            ref = piece(layer, groups[which], rows_of[layer], side)
            send(ref, ref, gs(layer), YS + which * 2 + side, at(dy=d))

    def y_wait(layer, which):
        for side in (0, 1):
            arrived(piece(layer, groups[which], other_of[layer], side), gs(layer), YS + which * 2 + side)

    def block(layer, group, core, rows):
        return bufs[layer].at[group, :, core, span(rows)]

    def c_send(layer, which, half):
        rows = (rows_of, other_of)[half][layer]
        ref = block(layer, groups[which], c, rows)
        send(ref, ref, gs(layer), CS + which * 2 + half, at(dc=1))

    def c_wait(layer, which):
        for half in (0, 1):
            rows = (rows_of, other_of)[half][layer]
            arrived(block(layer, groups[which], 1 - c, rows), gs(layer), CS + which * 2 + half)

    z_send(0)
    x_send(0, 0)
    z_send(1)
    x_send(1, 0)
    hs = (hsend, hrecv)
    send(frames.at[0, pl.ds(ROWS - EDGE, EDGE)], xbuf.at[pl.ds(0, EDGE)], hs, 0, right)
    send(frames.at[0, pl.ds(0, EDGE)], xbuf.at[pl.ds(EDGE + ROWS, EDGE)], hs, 1, left)

    def norm(start, size):
        values = xbuf[pl.ds(start, size), :].astype(F32)
        centre = jnp.mean(values, axis=-1, keepdims=True)
        deviate = values - centre
        spread = jnp.mean(deviate * deviate, axis=-1, keepdims=True)
        normed = (deviate * lax.rsqrt(spread + 1e-05) * ln_gain[...]).astype(BF16)
        for g in range(3):
            nbuf[g, pl.ds(start, size), :] = normed[:, g * 512:(g + 1) * 512]

    own_frames.wait()

    def norm_step(i, carry):
        norm(pl.multiple_of(EDGE + i * 32, 16), 32)
        return carry

    lax.fori_loop(0, ROWS // 32, norm_step, 0)
    arrived(xbuf.at[pl.ds(0, EDGE)], hs, 0)
    norm(0, EDGE)
    arrived(xbuf.at[pl.ds(EDGE + ROWS, EDGE)], hs, 1)
    norm(EDGE + ROWS, EDGE)

    own_rows[0].wait()
    own_rows[1].wait()
    x_wait(0, 0)
    y_send(0, 0)
    z_wait(0)
    x_send(0, 1)
    x_send(0, 2)
    x_wait(1, 0)
    y_send(1, 0)
    c_send(0, 0, 0)
    c_send(1, 0, 0)
    z_wait(1)
    x_send(1, 1)
    x_send(1, 2)
    for which in (1, 2):
        x_wait(0, which)
        y_send(0, which)
        c_send(0, which, 0)
    z_send(2)
    x_send(2, 0)
    for layer in (0, 1):
        y_wait(layer, 0)
        c_send(layer, 0, 1)
    for which in (1, 2):
        x_wait(1, which)
        y_send(1, which)
        c_send(1, which, 0)
    for layer in (0, 1):
        c_wait(layer, 0)

    def dot(g, m, size, cols):
        w = wbuf[g, :, :, :, cols].reshape(512, 256)
        return jnp.dot(nbuf[g, pl.ds(m, size), :], w, preferred_element_type=F32)

    def first_dot(j, carry):
        cols = pl.ds(pl.multiple_of(j * 256, 256), 256)
        acc[j] = dot(zh, 0, ALL, cols)
        return carry

    lax.fori_loop(0, 6, first_dot, 0)
    for layer in (0, 1):
        for which in (1, 2):
            y_wait(layer, which)
            c_send(layer, which, 1)
    z_wait(2)
    x_send(2, 1)
    x_send(2, 2)
    own_rows[2].wait()
    x_wait(2, 0)
    y_send(2, 0)
    c_send(2, 0, 0)
    for layer in (0, 1):
        for which in (1, 2):
            c_wait(layer, which)

    length = lengths[0]
    HM = ALL // 2

    def gate_step(i, carry):
        j, m = i // 2, i % 2
        m0 = pl.multiple_of(m * HM, 16)
        position = t * ROWS - EDGE + m0 + lax.broadcasted_iota(jnp.int32, (HM, 256), 0)
        valid = (position >= 0) & (position < length)
        pair = []
        for k in (0, 3):
            cols = pl.ds(pl.multiple_of((j + k) * 256, 256), 256)
            pair.append(acc[j + k, pl.ds(m0, HM), :] + (dot(up, m0, HM, cols) + dot(down, m0, HM, cols)))
        gated = jnp.where(valid, pair[0] * sigmoid(pair[1]), 0.0).astype(BF16).astype(F32)
        gbuf[j * 2, pl.ds(m0, HM), :] = gated[:, :128]
        gbuf[j * 2 + 1, pl.ds(m0, HM), :] = gated[:, 128:]
        return carry

    lax.fori_loop(0, 6, gate_step, 0)

    for which in (1, 2):
        x_wait(2, which)
        y_send(2, which)
        c_send(2, which, 0)

    local = jnp.clip(length - t * ROWS, 0, ROWS).astype(F32)
    BLOCK = 64

    def conv_step(s, carry):
        lanes = pl.ds(pl.multiple_of(s * 128, 128), 128)
        total = jnp.zeros((8, 128), F32)
        for b in range(0, ROWS, BLOCK):
            value = jnp.zeros((BLOCK, 128), F32)
            for k in range(TAPS):
                value = value + gbuf[s, pl.ds(b + 1 + k, BLOCK), :] * dw[pl.ds(k, 1), lanes]
            cbuf[s, pl.ds(b, BLOCK), :] = value
            position = t * ROWS + b + lax.broadcasted_iota(jnp.int32, (BLOCK, 128), 0)
            masked = jnp.where(position < length, value, 0.0)
            total = total + masked.reshape(BLOCK // 8, 8, 128).sum(axis=0)
        mean = total.sum(axis=0, keepdims=True) / jnp.maximum(local, 1.0)
        square = jnp.zeros((8, 128), F32)
        for b in range(0, ROWS, BLOCK):
            position = t * ROWS + b + lax.broadcasted_iota(jnp.int32, (BLOCK, 128), 0)
            delta = jnp.where(position < length, cbuf[s, pl.ds(b, BLOCK), :] - mean, 0.0)
            square = square + (delta * delta).reshape(BLOCK // 8, 8, 128).sum(axis=0)
        r1[slot1, pl.ds(s, 1), :] = mean
        r1[slot1, pl.ds(s + 8, 1), :] = square.sum(axis=0, keepdims=True)
        return carry

    r1[slot1] = jnp.zeros((16, 128), F32)
    lax.fori_loop(0, STRIPS, conv_step, 0)
    r1[slot1, pl.ds(6, 1), :] = jnp.full((1, 128), local, F32)

    def exchange(ref, slot, count, base, to):
        sems = (ssend, srecv)
        for d in range(1, count):
            send(ref.at[slot], ref.at[slot], sems, base + d, to(d))
        for d in range(1, count):
            arrived(ref.at[(slot + count - d) % count], sems, base + d)
        return combine(ref, count)

    mean, square = exchange(r1, slot1, 8, 0, peer1)
    r2[y, 0:8, :] = mean
    r2[y, 8:16, :] = square
    for which in (0, 1, 2):
        y_wait(2, which)
        c_send(2, which, 1)
    mean, square = exchange(r2, y, NY, 8, lambda d: at(dy=d))
    r3[z, 0:8, :] = mean
    r3[z, 8:16, :] = square
    mean, square = exchange(r3, z, NZ, 16, lambda d: at(dz=d))
    count = mean[6:7, :]
    scale = lax.rsqrt(square / count + 1e-05)
    for which in (0, 1, 2):
        c_wait(2, which)

    TM = 128
    final[0:8, :] = mean
    final[8:16, :] = scale

    def last_step(i, carry):
        m0 = pl.multiple_of(i * TM, TM)
        for s in range(STRIPS):
            lanes = slice(s * 128, (s + 1) * 128)
            factor = final[8 + s:9 + s, :] * bn_gain[:, lanes]
            value = (cbuf[s, pl.ds(m0, TM), :] - final[s:s + 1, :]) * factor + bn_shift[:, lanes]
            act[:, lanes] = (value * sigmoid(value)).astype(BF16)
        position = t * ROWS + m0 + lax.broadcasted_iota(jnp.int32, (TM, 512), 0)
        valid = position < length
        for j in range(3):
            w = vbuf[:, :, :, :, j * 512:(j + 1) * 512].reshape(CH, 512)
            res = jnp.dot(act[...], w, preferred_element_type=F32)
            out[0, pl.ds(m0, TM), j * 512:(j + 1) * 512] = jnp.where(valid, res, 0.0).astype(BF16)
        return carry

    lax.fori_loop(0, ROWS // TM, last_step, 0)
    for copy in sent:
        copy.wait_send()


def body(frames, lengths, ln_gain, w_in, dw_kernel, bn_gain, bn_shift, w_out):
    hbm = pl.BlockSpec(memory_space=pltpu.HBM)
    vmem = pl.BlockSpec(memory_space=pltpu.VMEM)
    smem = pl.BlockSpec(memory_space=pltpu.SMEM)
    return pl.pallas_call(
        kernel,
        out_shape=jax.ShapeDtypeStruct((1, ROWS, D), BF16),
        in_specs=[hbm, smem, vmem, hbm, vmem, vmem, vmem, hbm],
        out_specs=vmem,
        scratch_shapes=[
            pltpu.VMEM((ALL, D), BF16),
            pltpu.VMEM((3, ALL, 512), BF16),
            pltpu.VMEM((3, NX, 2, 64, D), BF16),
            pltpu.VMEM((3, NX, 2, 32, D), BF16),
            pltpu.VMEM((6, ALL, 256), F32),
            pltpu.VMEM((STRIPS, ALL, 128), F32),
            pltpu.VMEM((STRIPS, ROWS, 128), F32),
            pltpu.VMEM((128, CH), BF16),
            pltpu.VMEM((8, 16, 128), F32),
            pltpu.VMEM((NY, 16, 128), F32),
            pltpu.VMEM((NZ, 16, 128), F32),
            pltpu.VMEM((16, 128), F32),
            pltpu.SemaphoreType.DMA((LAYERS, SEMS)),
            pltpu.SemaphoreType.DMA((LAYERS, SEMS)),
            pltpu.SemaphoreType.DMA((2,)),
            pltpu.SemaphoreType.DMA((2,)),
            pltpu.SemaphoreType.DMA((28,)),
            pltpu.SemaphoreType.DMA((28,)),
            pltpu.SemaphoreType.DMA((4,)),
        ],
        compiler_params=pltpu.CompilerParams(
            collective_id=0, has_side_effects=True, vmem_limit_bytes=50 << 20
        ),
        name="conformer_conv",
    )(frames, lengths, ln_gain.reshape(1, D), w_in, dw_kernel, bn_gain.reshape(1, CH), bn_shift.reshape(1, CH), w_out)


def solution(mesh):
    return jax.shard_map(
        body,
        mesh=mesh,
        in_specs=(
            P("fsdp", "ctx", None),
            P("fsdp"),
            P(),
            P("fsdp", None),
            P(),
            P(),
            P(),
            P("fsdp", None),
        ),
        out_specs=P("fsdp", "ctx", None),
        check_vma=False,
    )
```

```python
import jax
import jax.numpy as jnp
from jax import lax
from jax.experimental import pallas as pl
from jax.experimental.pallas import tpu as pltpu
from jax.sharding import PartitionSpec as P

MESH = pl.DeviceIdType.MESH
BF16 = jnp.bfloat16
F32 = jnp.float32
NX, NY, NZ = 4, 8, 12
ROWS, EDGE = 512, 16
ALL = ROWS + 2 * EDGE
TAPS, CH, D = 31, 768, 1536
STRIPS = CH // 128
LAYERS = 3
ZS, XS, YS = 0, 2, 8
XO, CS = 0, 3


def device_of(x, y, z, c):
    return (((z // 4) * NX + x) * 2 + c, (z % 4) * NY + y)


def sigmoid(v):
    return 0.5 * jnp.tanh(0.5 * v) + 0.5


def combine(all_ref, parts):
    means = [all_ref[i, 0:8, :] for i in range(parts)]
    counts = [all_ref[i, 6:7, :] for i in range(parts)]
    squares = [all_ref[i, 8:16, :] for i in range(parts)]
    total = sum(counts[1:], counts[0])
    inverse = 1.0 / jnp.maximum(total, 1.0)
    weighted = [m * n for m, n in zip(means, counts)]
    mean = sum(weighted[1:], weighted[0]) * inverse
    spread = sum(squares[1:], squares[0])
    for m, n in zip(means, counts):
        spread = spread + n * (m - mean) * (m - mean)
    row = lax.broadcasted_iota(jnp.int32, (8, 128), 0)
    mean = jnp.where(row == 6, jnp.broadcast_to(total, (8, 128)), mean)
    return mean, spread


def kernel(
    frames, lengths, ln_gain, w_in, dw, bn_gain, bn_shift, w_out, out,
    xbuf, nbuf, wbuf, vbuf, acc, gbuf, cbuf, act, r1, r2, r3, final,
    gsend, grecv, qsend, qrecv, hsend, hrecv, ssend, srecv, lsem,
):
    f, t = lax.axis_index("fsdp"), lax.axis_index("ctx")
    x, c = (f // 2) % NX, f % 2
    y = t % NY
    zh, zl = f // (2 * NX), t // NY
    z = zh * 4 + zl
    par = y % 2
    up, down = (zh + 1) % 3, (zh + 2) % 3
    groups = (zh, up, down)

    def at(dx=0, dy=0, dz=0, dc=0):
        return device_of((x + dx) % NX, (y + dy) % NY, (z + dz) % NZ, (c + dc) % 2)

    left, right = (f, (t + 31) % 32), (f, (t + 1) % 32)
    slot1 = x * 2 + c

    def peer1(d):
        to = (slot1 + d) % 8
        return device_of(to // 2, y, z, to % 2)

    peers = [left, right]
    peers += [peer1(d) for d in range(1, 8)]
    peers += [at(dy=d) for d in range(1, NY)]
    peers += [at(dz=d) for d in range(1, NZ)]

    rows_of = [par * 32, par * 32 + 16, par * 16]
    other_of = [(1 - par) * 32, (1 - par) * 32 + 16, (1 - par) * 16]
    bufs = [wbuf, wbuf, vbuf]
    shards = [w_in, w_in, w_out]

    def span(start):
        return pl.ds(pl.multiple_of(start, 16), 16)

    own_frames = pltpu.make_async_copy(frames.at[0], xbuf.at[pl.ds(EDGE, ROWS)], lsem.at[0])
    own_frames.start()
    own_rows = []
    for layer in range(LAYERS):
        copy = pltpu.make_async_copy(
            shards[layer].at[span(rows_of[layer])],
            bufs[layer].at[zh, x, c, span(rows_of[layer])],
            lsem.at[1 + layer],
        )
        copy.start()
        own_rows.append(copy)

    barrier = pltpu.get_barrier_semaphore()
    for peer in peers:
        pl.semaphore_signal(barrier, inc=1, device_id=peer, device_id_type=MESH)
    pl.semaphore_wait(barrier, len(peers))

    sent = []

    def remote(src, dst, sems, k, to):
        return pltpu.make_async_remote_copy(
            src_ref=src, dst_ref=dst, send_sem=sems[0].at[k], recv_sem=sems[1].at[k],
            device_id=to, device_id_type=MESH,
        )

    def send(*args):
        copy = remote(*args)
        copy.start()
        sent.append(copy)

    def arrived(dst, sems, k):
        remote(dst, dst, sems, k, at(dc=1)).wait_recv()

    def gs(chunk):
        return (gsend.at[chunk], grecv.at[chunk])

    def qs(layer):
        return (qsend.at[layer], qrecv.at[layer])

    XD = (1, 3, 2)

    def half(chunk):
        return pl.ds((chunk % 2) * CH, CH)

    def unit(chunk, group, xs):
        layer = chunk // 2
        return bufs[layer].at[group, xs, c, span(rows_of[layer]), half(chunk)]

    def z_send(chunk):
        src = shards[chunk // 2].at[span(rows_of[chunk // 2]), half(chunk)]
        dst = unit(chunk, zh, x)
        send(src, dst, gs(chunk), ZS + 0, at(dz=-4))
        send(src, dst, gs(chunk), ZS + 1, at(dz=4))

    def z_wait(chunk):
        arrived(unit(chunk, up, x), gs(chunk), ZS + 0)
        arrived(unit(chunk, down, x), gs(chunk), ZS + 1)

    def xo_send(layer):
        src = shards[layer].at[span(rows_of[layer])]
        dst = bufs[layer].at[zh, x, c, span(rows_of[layer])]
        for i, d in enumerate(XD):
            send(src, dst, qs(layer), XO + i, at(dx=d))

    def xo_wait(layer):
        for i, d in enumerate(XD):
            dst = bufs[layer].at[zh, (x + 4 - d) % NX, c, span(rows_of[layer])]
            arrived(dst, qs(layer), XO + i)

    def xf_send(chunk):
        for which in (1, 2):
            ref = unit(chunk, groups[which], x)
            for i, d in enumerate(XD):
                send(ref, ref, gs(chunk), XS + (which - 1) * 3 + i, at(dx=d))

    def xf_wait(chunk):
        for which in (1, 2):
            for i, d in enumerate(XD):
                ref = unit(chunk, groups[which], (x + 4 - d) % NX)
                arrived(ref, gs(chunk), XS + (which - 1) * 3 + i)

    def piece(chunk, which, rows):
        layer = chunk // 2
        return bufs[layer].at[groups[which], :, c, span(rows[layer]), half(chunk)]

    def y_send(chunk, which):
        ref = piece(chunk, which, rows_of)
        send(ref, ref, gs(chunk), YS + which, at(dy=(1, 7)[chunk % 2]))

    def y_wait(chunk, which):
        arrived(piece(chunk, which, other_of), gs(chunk), YS + which)

    def c_send(layer, which, part):
        rows = (rows_of, other_of)[part][layer]
        ref = bufs[layer].at[groups[which], :, c, span(rows)]
        send(ref, ref, qs(layer), CS + which * 2 + part, at(dc=1))

    def c_wait(layer, which):
        for part in (0, 1):
            rows = (rows_of, other_of)[part][layer]
            ref = bufs[layer].at[groups[which], :, 1 - c, span(rows)]
            arrived(ref, qs(layer), CS + which * 2 + part)

    z_send(0)
    z_send(1)
    xo_send(0)
    xo_send(1)
    hs = (hsend, hrecv)
    send(frames.at[0, pl.ds(ROWS - EDGE, EDGE)], xbuf.at[pl.ds(0, EDGE)], hs, 0, right)
    send(frames.at[0, pl.ds(0, EDGE)], xbuf.at[pl.ds(EDGE + ROWS, EDGE)], hs, 1, left)

    def norm(start, size):
        values = xbuf[pl.ds(start, size), :].astype(F32)
        centre = jnp.mean(values, axis=-1, keepdims=True)
        deviate = values - centre
        spread = jnp.mean(deviate * deviate, axis=-1, keepdims=True)
        normed = (deviate * lax.rsqrt(spread + 1e-05) * ln_gain[...].reshape(1, D)).astype(BF16)
        for g in range(3):
            nbuf[g, pl.ds(start, size), :] = normed[:, g * 512:(g + 1) * 512]

    own_frames.wait()

    def norm_step(i, carry):
        norm(pl.multiple_of(EDGE + i * 32, 16), 32)
        return carry

    lax.fori_loop(0, ROWS // 32, norm_step, 0)
    arrived(xbuf.at[pl.ds(0, EDGE)], hs, 0)
    norm(0, EDGE)
    arrived(xbuf.at[pl.ds(EDGE + ROWS, EDGE)], hs, 1)
    norm(EDGE + ROWS, EDGE)

    def dot(g, m, size, cols):
        w = wbuf[g, :, :, :, cols].reshape(512, 256)
        return jnp.dot(nbuf[g, pl.ds(m, size), :], w, preferred_element_type=F32)

    def first_dot(j, carry):
        cols = pl.ds(pl.multiple_of(j * 256, 256), 256)
        acc[j] = dot(zh, 0, ALL, cols)
        return carry

    z_wait(0)
    z_send(2)
    xf_send(0)
    own_rows[0].wait()
    own_rows[1].wait()
    xo_wait(0)
    xo_wait(1)
    for chunk in range(4):
        y_send(chunk, 0)
    z_wait(1)
    z_send(3)
    xf_send(1)
    c_send(0, 0, 0)
    c_send(1, 0, 0)
    z_wait(2)
    xf_send(2)
    xf_wait(0)
    y_send(0, 1)
    y_send(0, 2)
    z_wait(3)
    xf_send(3)
    z_send(4)
    z_send(5)
    xf_wait(1)
    y_send(1, 1)
    y_send(1, 2)
    c_send(0, 1, 0)
    c_send(0, 2, 0)
    for chunk in range(4):
        y_wait(chunk, 0)
    c_send(0, 0, 1)
    c_send(1, 0, 1)
    xf_wait(2)
    y_send(2, 1)
    y_send(2, 2)
    xo_send(2)
    for layer in (0, 1):
        c_wait(layer, 0)
    lax.fori_loop(0, 6, first_dot, 0)
    xf_wait(3)
    for which in (1, 2):
        y_send(3, which)
        c_send(1, which, 0)
    for layer in (0, 1):
        for which in (1, 2):
            y_wait(2 * layer, which)
            y_wait(2 * layer + 1, which)
            c_send(layer, which, 1)
    z_wait(4)
    z_wait(5)
    xf_send(4)
    xf_send(5)
    own_rows[2].wait()
    xo_wait(2)
    y_send(4, 0)
    y_send(5, 0)
    c_send(2, 0, 0)
    for layer in (0, 1):
        for which in (1, 2):
            c_wait(layer, which)

    length = lengths[0]
    HM = ALL // 2

    def gate_step(i, carry):
        j, m = i // 2, i % 2
        m0 = pl.multiple_of(m * HM, 16)
        position = t * ROWS - EDGE + m0 + lax.broadcasted_iota(jnp.int32, (HM, 256), 0)
        valid = (position >= 0) & (position < length)
        pair = []
        for k in (0, 3):
            cols = pl.ds(pl.multiple_of((j + k) * 256, 256), 256)
            pair.append(acc[j + k, pl.ds(m0, HM), :] + (dot(up, m0, HM, cols) + dot(down, m0, HM, cols)))
        gated = jnp.where(valid, pair[0] * sigmoid(pair[1]), 0.0).astype(BF16).astype(F32)
        gbuf[j * 2, pl.ds(m0, HM), :] = gated[:, :128]
        gbuf[j * 2 + 1, pl.ds(m0, HM), :] = gated[:, 128:]
        return carry

    lax.fori_loop(0, 6, gate_step, 0)

    xf_wait(4)
    xf_wait(5)
    for which in (1, 2):
        y_send(4, which)
        y_send(5, which)
        c_send(2, which, 0)

    local = jnp.clip(length - t * ROWS, 0, ROWS).astype(F32)
    BLOCK = 64

    def conv_step(s, carry):
        lanes = pl.ds(pl.multiple_of(s * 128, 128), 128)
        total = jnp.zeros((8, 128), F32)
        for b in range(0, ROWS, BLOCK):
            value = jnp.zeros((BLOCK, 128), F32)
            for k in range(TAPS):
                value = value + gbuf[s, pl.ds(b + 1 + k, BLOCK), :] * dw[pl.ds(k, 1), lanes]
            cbuf[s, pl.ds(b, BLOCK), :] = value
            position = t * ROWS + b + lax.broadcasted_iota(jnp.int32, (BLOCK, 128), 0)
            masked = jnp.where(position < length, value, 0.0)
            total = total + masked.reshape(BLOCK // 8, 8, 128).sum(axis=0)
        mean = total.sum(axis=0, keepdims=True) / jnp.maximum(local, 1.0)
        square = jnp.zeros((8, 128), F32)
        for b in range(0, ROWS, BLOCK):
            position = t * ROWS + b + lax.broadcasted_iota(jnp.int32, (BLOCK, 128), 0)
            delta = jnp.where(position < length, cbuf[s, pl.ds(b, BLOCK), :] - mean, 0.0)
            square = square + (delta * delta).reshape(BLOCK // 8, 8, 128).sum(axis=0)
        r1[slot1, pl.ds(s, 1), :] = mean
        r1[slot1, pl.ds(s + 8, 1), :] = square.sum(axis=0, keepdims=True)
        return carry

    r1[slot1] = jnp.zeros((16, 128), F32)
    lax.fori_loop(0, STRIPS, conv_step, 0)
    r1[slot1, pl.ds(6, 1), :] = jnp.full((1, 128), local, F32)

    def exchange(ref, slot, count, base, to):
        sems = (ssend, srecv)
        for d in range(1, count):
            send(ref.at[slot], ref.at[slot], sems, base + d, to(d))
        for d in range(1, count):
            arrived(ref.at[(slot + count - d) % count], sems, base + d)
        return combine(ref, count)

    mean, square = exchange(r1, slot1, 8, 0, peer1)
    r2[y, 0:8, :] = mean
    r2[y, 8:16, :] = square
    for which in (0, 1, 2):
        y_wait(4, which)
        y_wait(5, which)
        c_send(2, which, 1)
    mean, square = exchange(r2, y, NY, 8, lambda d: at(dy=d))
    r3[z, 0:8, :] = mean
    r3[z, 8:16, :] = square
    mean, square = exchange(r3, z, NZ, 16, lambda d: at(dz=d))
    count = mean[6:7, :]
    scale = lax.rsqrt(square / count + 1e-05)
    for which in (0, 1, 2):
        c_wait(2, which)

    TM = 128
    final[0:8, :] = mean
    final[8:16, :] = scale

    def last_step(i, carry):
        m0 = pl.multiple_of(i * TM, TM)
        for s in range(STRIPS):
            lanes = slice(s * 128, (s + 1) * 128)
            factor = final[8 + s:9 + s, :] * bn_gain[lanes].reshape(1, 128)
            value = (cbuf[s, pl.ds(m0, TM), :] - final[s:s + 1, :]) * factor + bn_shift[lanes].reshape(1, 128)
            act[:, lanes] = (value * sigmoid(value)).astype(BF16)
        position = t * ROWS + m0 + lax.broadcasted_iota(jnp.int32, (TM, 512), 0)
        valid = position < length
        for j in range(3):
            w = vbuf[:, :, :, :, j * 512:(j + 1) * 512].reshape(CH, 512)
            res = jnp.dot(act[...], w, preferred_element_type=F32)
            out[0, pl.ds(m0, TM), j * 512:(j + 1) * 512] = jnp.where(valid, res, 0.0).astype(BF16)
        return carry

    lax.fori_loop(0, ROWS // TM, last_step, 0)
    for copy in sent:
        copy.wait_send()


def body(frames, lengths, ln_gain, w_in, dw_kernel, bn_gain, bn_shift, w_out):
    hbm = pl.BlockSpec(memory_space=pltpu.HBM)
    vmem = pl.BlockSpec(memory_space=pltpu.VMEM)
    smem = pl.BlockSpec(memory_space=pltpu.SMEM)
    return pl.pallas_call(
        kernel,
        out_shape=jax.ShapeDtypeStruct((1, ROWS, D), BF16),
        in_specs=[hbm, smem, vmem, hbm, vmem, vmem, vmem, hbm],
        out_specs=vmem,
        scratch_shapes=[
            pltpu.VMEM((ALL, D), BF16),
            pltpu.VMEM((3, ALL, 512), BF16),
            pltpu.VMEM((3, NX, 2, 64, D), BF16),
            pltpu.VMEM((3, NX, 2, 32, D), BF16),
            pltpu.VMEM((6, ALL, 256), F32),
            pltpu.VMEM((STRIPS, ALL, 128), F32),
            pltpu.VMEM((STRIPS, ROWS, 128), F32),
            pltpu.VMEM((128, CH), BF16),
            pltpu.VMEM((8, 16, 128), F32),
            pltpu.VMEM((NY, 16, 128), F32),
            pltpu.VMEM((NZ, 16, 128), F32),
            pltpu.VMEM((16, 128), F32),
            pltpu.SemaphoreType.DMA((2 * LAYERS, 11)),
            pltpu.SemaphoreType.DMA((2 * LAYERS, 11)),
            pltpu.SemaphoreType.DMA((LAYERS, 9)),
            pltpu.SemaphoreType.DMA((LAYERS, 9)),
            pltpu.SemaphoreType.DMA((2,)),
            pltpu.SemaphoreType.DMA((2,)),
            pltpu.SemaphoreType.DMA((28,)),
            pltpu.SemaphoreType.DMA((28,)),
            pltpu.SemaphoreType.DMA((4,)),
        ],
        compiler_params=pltpu.CompilerParams(
            collective_id=0, has_side_effects=True, vmem_limit_bytes=63 << 20
        ),
        name="conformer_conv",
    )(frames, lengths, ln_gain, w_in, dw_kernel, bn_gain, bn_shift, w_out)


def solution(mesh):
    return jax.shard_map(
        body,
        mesh=mesh,
        in_specs=(
            P("fsdp", "ctx", None),
            P("fsdp"),
            P(),
            P("fsdp", None),
            P(),
            P(),
            P(),
            P("fsdp", None),
        ),
        out_specs=P("fsdp", "ctx", None),
        check_vma=False,
    )
```

```python
import jax
import jax.numpy as jnp
from jax import lax
from jax.experimental import pallas as pl
from jax.experimental.pallas import tpu as pltpu
from jax.sharding import PartitionSpec as P

MESH = pl.DeviceIdType.MESH
BF16 = jnp.bfloat16
F32 = jnp.float32
NX, NY, NZ = 4, 8, 12
ROWS, EDGE = 512, 16
ALL = ROWS + 2 * EDGE
TAPS, CH, D = 31, 768, 1536
STRIPS = CH // 128


def device_of(x, y, z, c):
    return (((z // 4) * NX + x) * 2 + c, (z % 4) * NY + y)


def sigmoid(v):
    return 0.5 * jnp.tanh(0.5 * v) + 0.5


def combine(all_ref, parts):
    means = [all_ref[i, 0:8, :] for i in range(parts)]
    counts = [all_ref[i, 6:7, :] for i in range(parts)]
    squares = [all_ref[i, 8:16, :] for i in range(parts)]
    total = sum(counts[1:], counts[0])
    inverse = 1.0 / jnp.maximum(total, 1.0)
    weighted = [m * n for m, n in zip(means, counts)]
    mean = sum(weighted[1:], weighted[0]) * inverse
    spread = sum(squares[1:], squares[0])
    for m, n in zip(means, counts):
        spread = spread + n * (m - mean) * (m - mean)
    row = lax.broadcasted_iota(jnp.int32, (8, 128), 0)
    mean = jnp.where(row == 6, jnp.broadcast_to(total, (8, 128)), mean)
    return mean, spread


def kernel(
    frames, lengths, ln_gain, w_in, dw, bn_gain, bn_shift, w_out, out,
    xbuf, nbuf, wbuf, vbuf, acc, gbuf, cbuf, act, r1, r2, r3, final,
    gsend, grecv, qsend, qrecv, vsend, vrecv, hsend, hrecv, ssend, srecv, lsem,
):
    f, t = lax.axis_index("fsdp"), lax.axis_index("ctx")
    x, c = (f // 2) % NX, f % 2
    y = t % NY
    zh, zl = f // (2 * NX), t // NY
    z = zh * 4 + zl
    par = y % 2
    up, down = (zh + 1) % 3, (zh + 2) % 3
    groups = (zh, up, down)

    def at(dx=0, dy=0, dz=0, dc=0):
        return device_of((x + dx) % NX, (y + dy) % NY, (z + dz) % NZ, (c + dc) % 2)

    left, right = (f, (t + 31) % 32), (f, (t + 1) % 32)
    slot1 = x * 2 + c

    def peer1(d):
        to = (slot1 + d) % 8
        return device_of(to // 2, y, z, to % 2)

    peers = [left, right]
    peers += [peer1(d) for d in range(1, 8)]
    peers += [at(dy=d) for d in range(1, NY)]
    peers += [at(dz=d) for d in range(1, NZ)]

    mine_in = pl.ds(pl.multiple_of(par * 32, 32), 32)
    other_in = pl.ds(pl.multiple_of((1 - par) * 32, 32), 32)
    mine_out = pl.ds(pl.multiple_of(par * 16, 16), 16)
    other_out = pl.ds(pl.multiple_of((1 - par) * 16, 16), 16)
    direct, split = pl.ds(0, 3), pl.ds(3, 3)
    far = pl.ds(1, 2)

    own_frames = pltpu.make_async_copy(frames.at[0], xbuf.at[pl.ds(EDGE, ROWS)], lsem.at[0])
    own_frames.start()
    own_in, own_out = [], []
    for j in range(STRIPS):
        for side in (0, 1):
            cols = pl.ds(side * CH + j * 128, 128)
            src, dst = w_in.at[:, cols], wbuf.at[0, x, c, j, side]
            if j >= 3:
                src, dst = w_in.at[mine_in, cols], wbuf.at[0, x, c, j, side, mine_in]
            own_in.append(pltpu.make_async_copy(src, dst, lsem.at[1 + len(own_in)]))
    for side in (0, 1):
        src = w_out.at[mine_out, pl.ds(side * CH, CH)]
        own_out.append(pltpu.make_async_copy(src, vbuf.at[0, x, c, side, mine_out], lsem.at[13 + side]))
    for copy in own_in + own_out:
        copy.start()

    barrier = pltpu.get_barrier_semaphore()
    for peer in peers:
        pl.semaphore_signal(barrier, inc=1, device_id=peer, device_id_type=MESH)
    pl.semaphore_wait(barrier, len(peers))

    sent = []

    def remote(src, dst, sems, k, to):
        return pltpu.make_async_remote_copy(
            src_ref=src, dst_ref=dst, send_sem=sems[0].at[k], recv_sem=sems[1].at[k],
            device_id=to, device_id_type=MESH,
        )

    def send(*args):
        remote(*args).start()
        if args[2][0] is hsend or args[2][0] is ssend:
            sent.append(args)

    def arrived(dst, sems, k):
        remote(dst, dst, sems, k, at(dc=1)).wait_recv()

    XD = (1, 3, 2)

    def gs(j):
        return (gsend.at[j], grecv.at[j])

    qs = (qsend, qrecv)

    def z_send(j):
        src = wbuf.at[0, x, c, j, :, mine_in]
        send(src, wbuf.at[1, x, c, j, :, mine_in], gs(j), 0, at(dz=-4))
        send(src, wbuf.at[2, x, c, j, :, mine_in], gs(j), 1, at(dz=4))

    def z_wait(j):
        arrived(wbuf.at[1, x, c, j, :, mine_in], gs(j), 0)
        arrived(wbuf.at[2, x, c, j, :, mine_in], gs(j), 1)

    def x_send(j):
        ref = wbuf.at[far, x, c, j, :, mine_in]
        for i, d in enumerate(XD):
            send(ref, ref, gs(j), 2 + i, at(dx=d))

    def x_wait(j):
        for i, d in enumerate(XD):
            arrived(wbuf.at[far, (x + 4 - d) % NX, c, j, :, mine_in], gs(j), 2 + i)

    def y_send(j):
        for side, d in ((0, 1), (1, 7)):
            ref = wbuf.at[far, :, c, j, side, mine_in]
            send(ref, ref, gs(j), 5 + side, at(dy=d))

    def y_wait(j):
        for side in (0, 1):
            arrived(wbuf.at[far, :, c, j, side, other_in], gs(j), 5 + side)

    def c_send(j, part):
        ref = wbuf.at[far, :, c, j, :, (mine_in, other_in)[part]]
        send(ref, ref, gs(j), 7 + part, at(dc=1))

    def c_wait(j):
        for part in (0, 1):
            arrived(wbuf.at[far, :, 1 - c, j, :, (mine_in, other_in)[part]], gs(j), 7 + part)

    def xo_send():
        first, second = wbuf.at[0, x, c, direct], wbuf.at[0, x, c, split, :, mine_in]
        for i, d in enumerate(XD):
            send(first, first, qs, i, at(dx=d))
        for i, d in enumerate(XD):
            send(second, second, qs, 3 + i, at(dx=d))

    def xo_wait():
        for i, d in enumerate(XD):
            source = (x + 4 - d) % NX
            arrived(wbuf.at[0, source, c, direct], qs, i)
            arrived(wbuf.at[0, source, c, split, :, mine_in], qs, 3 + i)

    def own_y_send():
        for side, d in ((0, 1), (1, 7)):
            ref = wbuf.at[0, :, c, split, side, mine_in]
            send(ref, ref, qs, 6 + side, at(dy=d))

    def own_y_wait():
        for side in (0, 1):
            arrived(wbuf.at[0, :, c, split, side, other_in], qs, 6 + side)

    def own_part(part, core):
        if part == 0:
            return wbuf.at[0, :, core, direct]
        return wbuf.at[0, :, core, split, :, (mine_in, other_in)[part - 1]]

    def own_c_send(part):
        ref = own_part(part, c)
        send(ref, ref, qs, 8 + part, at(dc=1))

    def own_c_wait():
        for part in (0, 1, 2):
            arrived(own_part(part, 1 - c), qs, 8 + part)

    vs = (vsend, vrecv)

    def v_start():
        src = vbuf.at[0, x, c, :, mine_out]
        send(src, vbuf.at[1, x, c, :, mine_out], vs, 0, at(dz=-4))
        send(src, vbuf.at[2, x, c, :, mine_out], vs, 1, at(dz=4))
        for i, d in enumerate(XD):
            send(src, src, vs, 2 + i, at(dx=d))

    def v_x_send():
        arrived(vbuf.at[1, x, c, :, mine_out], vs, 0)
        arrived(vbuf.at[2, x, c, :, mine_out], vs, 1)
        ref = vbuf.at[far, x, c, :, mine_out]
        for i, d in enumerate(XD):
            send(ref, ref, vs, 5 + i, at(dx=d))

    def v_y_send():
        for i, d in enumerate(XD):
            source = (x + 4 - d) % NX
            arrived(vbuf.at[0, source, c, :, mine_out], vs, 2 + i)
            arrived(vbuf.at[far, source, c, :, mine_out], vs, 5 + i)
        for side, d in ((0, 1), (1, 7)):
            ref = vbuf.at[:, :, c, side, mine_out]
            send(ref, ref, vs, 8 + side, at(dy=d))
        ref = vbuf.at[:, :, c, :, mine_out]
        send(ref, ref, vs, 10, at(dc=1))

    def v_c_send():
        for side in (0, 1):
            arrived(vbuf.at[:, :, c, side, other_out], vs, 8 + side)
        ref = vbuf.at[:, :, c, :, other_out]
        send(ref, ref, vs, 11, at(dc=1))

    def v_wait():
        arrived(vbuf.at[:, :, 1 - c, :, mine_out], vs, 10)
        arrived(vbuf.at[:, :, 1 - c, :, other_out], vs, 11)

    for copy in own_in + own_out:
        copy.wait()
    z_send(0)
    z_send(1)
    xo_send()
    hs = (hsend, hrecv)
    send(frames.at[0, pl.ds(ROWS - EDGE, EDGE)], xbuf.at[pl.ds(0, EDGE)], hs, 0, right)
    send(frames.at[0, pl.ds(0, EDGE)], xbuf.at[pl.ds(EDGE + ROWS, EDGE)], hs, 1, left)

    def norm(start, size):
        values = xbuf[pl.ds(start, size), :].astype(F32)
        centre = jnp.mean(values, axis=-1, keepdims=True)
        deviate = values - centre
        spread = jnp.mean(deviate * deviate, axis=-1, keepdims=True)
        normed = (deviate * lax.rsqrt(spread + 1e-05) * ln_gain[...].reshape(1, D)).astype(BF16)
        for g in range(3):
            nbuf[g, pl.ds(start, size), :] = normed[:, g * 512:(g + 1) * 512]

    own_frames.wait()

    def norm_step(i, carry):
        norm(pl.multiple_of(EDGE + i * 32, 16), 32)
        return carry

    lax.fori_loop(0, ROWS // 32, norm_step, 0)
    arrived(xbuf.at[pl.ds(0, EDGE)], hs, 0)
    norm(0, EDGE)
    arrived(xbuf.at[pl.ds(EDGE + ROWS, EDGE)], hs, 1)
    norm(EDGE + ROWS, EDGE)

    def dot(g, j, m, size):
        w = [wbuf[g, :, :, j, side].reshape(512, 128) for side in (0, 1)]
        rows = nbuf[(zh + g) % 3, pl.ds(m, size), :]
        return jnp.dot(rows, jnp.concatenate(w, axis=1), preferred_element_type=F32)

    def first_dot(j, carry):
        acc[j] = dot(0, j, 0, ALL)
        return carry

    length = lengths[0]
    HM = ALL // 2

    def gate_step(j):
        def half(m, carry):
            m0 = pl.multiple_of(m * HM, 16)
            position = t * ROWS - EDGE + m0 + lax.broadcasted_iota(jnp.int32, (HM, 128), 0)
            valid = (position >= 0) & (position < length)
            pair = acc[j, pl.ds(m0, HM), :] + (dot(1, j, m0, HM) + dot(2, j, m0, HM))
            gated = jnp.where(valid, pair[:, :128] * sigmoid(pair[:, 128:]), 0.0)
            gbuf[j, pl.ds(m0, HM), :] = gated.astype(BF16).astype(F32)
            return carry

        lax.fori_loop(0, 2, half, 0)

    local = jnp.clip(length - t * ROWS, 0, ROWS).astype(F32)
    BLOCK = 64

    def conv_step(s):
        lanes = pl.ds(pl.multiple_of(s * 128, 128), 128)
        total = jnp.zeros((8, 128), F32)
        for b in range(0, ROWS, BLOCK):
            value = jnp.zeros((BLOCK, 128), F32)
            for k in range(TAPS):
                value = value + gbuf[s, pl.ds(b + 1 + k, BLOCK), :] * dw[pl.ds(k, 1), lanes]
            cbuf[s, pl.ds(b, BLOCK), :] = value
            position = t * ROWS + b + lax.broadcasted_iota(jnp.int32, (BLOCK, 128), 0)
            masked = jnp.where(position < length, value, 0.0)
            total = total + masked.reshape(BLOCK // 8, 8, 128).sum(axis=0)
        mean = total.sum(axis=0, keepdims=True) / jnp.maximum(local, 1.0)
        square = jnp.zeros((8, 128), F32)
        for b in range(0, ROWS, BLOCK):
            position = t * ROWS + b + lax.broadcasted_iota(jnp.int32, (BLOCK, 128), 0)
            delta = jnp.where(position < length, cbuf[s, pl.ds(b, BLOCK), :] - mean, 0.0)
            square = square + (delta * delta).reshape(BLOCK // 8, 8, 128).sum(axis=0)
        r1[slot1, pl.ds(s, 1), :] = mean
        r1[slot1, pl.ds(s + 8, 1), :] = square.sum(axis=0, keepdims=True)

    r1[slot1] = jnp.zeros((16, 128), F32)

    X_LAG, Y_LAG, C_LAG = 3, 6, 7

    def pipeline(i, carry):
        @pl.when(i < STRIPS)
        def _():
            z_wait(i)
            x_send(i)

        @pl.when(i < STRIPS - 2)
        def _():
            z_send(i + 2)

        @pl.when((i >= X_LAG) & (i < STRIPS + X_LAG))
        def _():
            x_wait(i - X_LAG)
            y_send(i - X_LAG)
            c_send(i - X_LAG, 0)

        @pl.when(i == 2)
        def _():
            xo_wait()
            own_y_send()
            own_c_send(0)
            own_c_send(1)

        @pl.when(i == 6)
        def _():
            v_start()
            own_y_wait()
            own_c_send(2)

        @pl.when((i >= Y_LAG) & (i < STRIPS + Y_LAG))
        def _():
            y_wait(i - Y_LAG)
            c_send(i - Y_LAG, 1)

        @pl.when(i == 7)
        def _():
            own_c_wait()
            lax.fori_loop(0, STRIPS, first_dot, 0)

        @pl.when(i == 9)
        def _():
            v_x_send()

        @pl.when(i == 12)
        def _():
            v_y_send()

        @pl.when(i >= C_LAG)
        def _():
            j = i - C_LAG
            c_wait(j)
            gate_step(j)
            conv_step(j)

        return carry

    lax.fori_loop(0, STRIPS + C_LAG, pipeline, 0)
    r1[slot1, pl.ds(6, 1), :] = jnp.full((1, 128), local, F32)

    def exchange(ref, slot, count, base, to, between=None):
        sems = (ssend, srecv)
        for d in range(1, count):
            send(ref.at[slot], ref.at[slot], sems, base + d, to(d))
        if between is not None:
            between()
        for d in range(1, count):
            arrived(ref.at[(slot + count - d) % count], sems, base + d)
        return combine(ref, count)

    mean, square = exchange(r1, slot1, 8, 0, peer1)
    r2[y, 0:8, :] = mean
    r2[y, 8:16, :] = square
    mean, square = exchange(r2, y, NY, 8, lambda d: at(dy=d))
    r3[z, 0:8, :] = mean
    r3[z, 8:16, :] = square
    mean, square = exchange(r3, z, NZ, 16, lambda d: at(dz=d), v_c_send)
    count = mean[6:7, :]
    scale = lax.rsqrt(square / count + 1e-05)
    v_wait()

    TM = 128
    final[0:8, :] = mean
    final[8:16, :] = scale

    def last_step(i, carry):
        m0 = pl.multiple_of(i * TM, TM)
        for s in range(STRIPS):
            lanes = slice(s * 128, (s + 1) * 128)
            factor = final[8 + s:9 + s, :] * bn_gain[lanes].reshape(1, 128)
            value = (cbuf[s, pl.ds(m0, TM), :] - final[s:s + 1, :]) * factor + bn_shift[lanes].reshape(1, 128)
            act[s // 2, :, (s % 2) * 128:(s % 2 + 1) * 128] = (value * sigmoid(value)).astype(BF16)
        position = t * ROWS + m0 + lax.broadcasted_iota(jnp.int32, (TM, CH), 0)
        valid = position < length
        for side in (0, 1):
            res = 0.0
            for g in range(3):
                w = vbuf[g, :, :, side].reshape(256, CH)
                res = res + jnp.dot(act[(zh + g) % 3], w, preferred_element_type=F32)
            out[0, pl.ds(m0, TM), side * CH:(side + 1) * CH] = jnp.where(valid, res, 0.0).astype(BF16)
        return carry

    lax.fori_loop(0, ROWS // TM, last_step, 0)
    def drain(j, carry):
        src = wbuf.at[0, x, c, j, :, mine_in]
        for k in (0, 1):
            remote(src, src, gs(j), k, at(dc=1)).wait_send()
        for k in (2, 3, 4):
            ref = wbuf.at[far, x, c, j, :, mine_in]
            remote(ref, ref, gs(j), k, at(dc=1)).wait_send()
        for side in (0, 1):
            ref = wbuf.at[far, :, c, j, side, mine_in]
            remote(ref, ref, gs(j), 5 + side, at(dc=1)).wait_send()
        for part in (0, 1):
            ref = wbuf.at[far, :, c, j, :, (mine_in, other_in)[part]]
            remote(ref, ref, gs(j), 7 + part, at(dc=1)).wait_send()
        return carry

    lax.fori_loop(0, STRIPS, drain, 0)
    leaving = [(wbuf.at[0, x, c, direct], qs, k) for k in (0, 1, 2)]
    leaving += [(wbuf.at[0, x, c, split, :, mine_in], qs, k) for k in (3, 4, 5)]
    leaving += [(wbuf.at[0, :, c, split, side, mine_in], qs, 6 + side) for side in (0, 1)]
    leaving += [(own_part(part, c), qs, 8 + part) for part in (0, 1, 2)]
    leaving += [(vbuf.at[0, x, c, :, mine_out], vs, k) for k in range(5)]
    leaving += [(vbuf.at[far, x, c, :, mine_out], vs, k) for k in (5, 6, 7)]
    leaving += [(vbuf.at[:, :, c, side, mine_out], vs, 8 + side) for side in (0, 1)]
    leaving += [(vbuf.at[:, :, c, :, rows], vs, 10 + k) for k, rows in enumerate((mine_out, other_out))]
    for ref, sems, k in leaving:
        remote(ref, ref, sems, k, at(dc=1)).wait_send()
    for args in sent:
        remote(*args).wait_send()


def body(frames, lengths, ln_gain, w_in, dw_kernel, bn_gain, bn_shift, w_out):
    hbm = pl.BlockSpec(memory_space=pltpu.HBM)
    vmem = pl.BlockSpec(memory_space=pltpu.VMEM)
    smem = pl.BlockSpec(memory_space=pltpu.SMEM)
    return pl.pallas_call(
        kernel,
        out_shape=jax.ShapeDtypeStruct((1, ROWS, D), BF16),
        in_specs=[hbm, smem, vmem, hbm, vmem, vmem, vmem, hbm],
        out_specs=vmem,
        scratch_shapes=[
            pltpu.VMEM((ALL, D), BF16),
            pltpu.VMEM((3, ALL, 512), BF16),
            pltpu.VMEM((3, NX, 2, STRIPS, 2, 64, 128), BF16),
            pltpu.VMEM((3, NX, 2, 2, 32, CH), BF16),
            pltpu.VMEM((6, ALL, 256), F32),
            pltpu.VMEM((STRIPS, ALL, 128), F32),
            pltpu.VMEM((STRIPS, ROWS, 128), F32),
            pltpu.VMEM((3, 128, 256), BF16),
            pltpu.VMEM((8, 16, 128), F32),
            pltpu.VMEM((NY, 16, 128), F32),
            pltpu.VMEM((NZ, 16, 128), F32),
            pltpu.VMEM((16, 128), F32),
            pltpu.SemaphoreType.DMA((STRIPS, 9)),
            pltpu.SemaphoreType.DMA((STRIPS, 9)),
            pltpu.SemaphoreType.DMA((11,)),
            pltpu.SemaphoreType.DMA((11,)),
            pltpu.SemaphoreType.DMA((12,)),
            pltpu.SemaphoreType.DMA((12,)),
            pltpu.SemaphoreType.DMA((2,)),
            pltpu.SemaphoreType.DMA((2,)),
            pltpu.SemaphoreType.DMA((28,)),
            pltpu.SemaphoreType.DMA((28,)),
            pltpu.SemaphoreType.DMA((15,)),
        ],
        compiler_params=pltpu.CompilerParams(
            collective_id=0, has_side_effects=True, vmem_limit_bytes=63 << 20
        ),
        name="conformer_conv",
    )(frames, lengths, ln_gain, w_in, dw_kernel, bn_gain, bn_shift, w_out)


def solution(mesh):
    return jax.shard_map(
        body,
        mesh=mesh,
        in_specs=(
            P("fsdp", "ctx", None),
            P("fsdp"),
            P(),
            P("fsdp", None),
            P(),
            P(),
            P(),
            P("fsdp", None),
        ),
        out_specs=P("fsdp", "ctx", None),
        check_vma=False,
    )
```

```python
import jax
import jax.numpy as jnp
from jax import lax
from jax.experimental import pallas as pl
from jax.experimental.pallas import tpu as pltpu
from jax.sharding import PartitionSpec as P

MESH = pl.DeviceIdType.MESH
BF16 = jnp.bfloat16
F32 = jnp.float32
NX, NY, NZ = 4, 8, 12
ROWS, EDGE = 512, 16
ALL = ROWS + 2 * EDGE
TAPS, CH, D = 31, 768, 1536
STRIPS = CH // 128


def device_of(x, y, z, c):
    return (((z // 4) * NX + x) * 2 + c, (z % 4) * NY + y)


def sigmoid(v):
    return 0.5 * jnp.tanh(0.5 * v) + 0.5


def combine(all_ref, parts):
    tables = [all_ref[i] for i in range(parts)]
    counts = [all_ref[i, 3:4, :] for i in range(parts)]
    total = sum(counts[1:], counts[0])
    weighted = [m * n for m, n in zip(tables, counts)]
    mean = sum(weighted[1:], weighted[0]) / jnp.maximum(total, 1.0)
    added = [n * (m - mean) * (m - mean) for m, n in zip(tables, counts)]
    square = sum(tables[1:], tables[0]) + pltpu.roll(sum(added[1:], added[0]), 4, 0)
    row = lax.broadcasted_iota(jnp.int32, (8, 128), 0)
    rest = jnp.where(row == 7, 0.0, square)
    return jnp.where(row < 3, mean, jnp.where(row == 3, jnp.broadcast_to(total, (8, 128)), rest))


def kernel(
    frames, lengths, ln_gain, w_in, dw, w_out, conv, wide, stats,
    xbuf, nbuf, wbuf, vbuf, acc, gbuf, cbuf, pay, r1, r2, r3, final,
    gsend, grecv, qsend, qrecv, vsend, vrecv, hsend, hrecv, ssend, srecv, lsem, csem,
):
    f, t = lax.axis_index("fsdp"), lax.axis_index("ctx")
    x, c = (f // 2) % NX, f % 2
    y = t % NY
    zh, zl = f // (2 * NX), t // NY
    z = zh * 4 + zl
    par = y % 2
    up, down = (zh + 1) % 3, (zh + 2) % 3
    groups = (zh, up, down)

    def at(dx=0, dy=0, dz=0, dc=0):
        return device_of((x + dx) % NX, (y + dy) % NY, (z + dz) % NZ, (c + dc) % 2)

    left, right = (f, (t + 31) % 32), (f, (t + 1) % 32)
    slot1 = x * 2 + c

    def peer1(d):
        to = (slot1 + d) % 8
        return device_of(to // 2, y, z, to % 2)

    peers = [left, right]
    peers += [peer1(d) for d in range(1, 8)]
    peers += [at(dy=d) for d in range(1, NY)]
    peers += [at(dz=d) for d in range(1, NZ)]

    mine_in = pl.ds(pl.multiple_of(par * 32, 32), 32)
    other_in = pl.ds(pl.multiple_of((1 - par) * 32, 32), 32)
    mine_out = pl.ds(pl.multiple_of(par * 16, 16), 16)
    other_out = pl.ds(pl.multiple_of((1 - par) * 16, 16), 16)
    direct, split = pl.ds(0, 3), pl.ds(3, 3)
    far = pl.ds(1, 2)

    own_frames = pltpu.make_async_copy(frames.at[0], xbuf.at[pl.ds(EDGE, ROWS)], lsem.at[0])
    own_frames.start()
    own_in, own_out = [], []
    for j in range(STRIPS):
        for side in (0, 1):
            cols = pl.ds(side * CH + j * 128, 128)
            src, dst = w_in.at[:, cols], wbuf.at[0, x, c, j, side]
            if j >= 3:
                src, dst = w_in.at[mine_in, cols], wbuf.at[0, x, c, j, side, mine_in]
            own_in.append(pltpu.make_async_copy(src, dst, lsem.at[1 + len(own_in)]))
    for side in (0, 1):
        src = w_out.at[mine_out, pl.ds(side * CH, CH)]
        own_out.append(pltpu.make_async_copy(src, vbuf.at[0, x, c, side, mine_out], lsem.at[13 + side]))
    for copy in own_in + own_out:
        copy.start()

    barrier = pltpu.get_barrier_semaphore()
    for peer in peers:
        pl.semaphore_signal(barrier, inc=1, device_id=peer, device_id_type=MESH)
    pl.semaphore_wait(barrier, len(peers))

    sent = []

    def remote(src, dst, sems, k, to):
        return pltpu.make_async_remote_copy(
            src_ref=src, dst_ref=dst, send_sem=sems[0].at[k], recv_sem=sems[1].at[k],
            device_id=to, device_id_type=MESH,
        )

    def send(*args):
        remote(*args).start()
        if args[2][0] is hsend or args[2][0] is ssend:
            sent.append(args)

    def arrived(dst, sems, k):
        remote(dst, dst, sems, k, at(dc=1)).wait_recv()

    XD = (1, 3, 2)

    def gs(j):
        return (gsend.at[j], grecv.at[j])

    qs = (qsend, qrecv)

    def z_send(j):
        src = wbuf.at[0, x, c, j, :, mine_in]
        send(src, wbuf.at[1, x, c, j, :, mine_in], gs(j), 0, at(dz=-4))
        send(src, wbuf.at[2, x, c, j, :, mine_in], gs(j), 1, at(dz=4))

    def z_wait(j):
        arrived(wbuf.at[1, x, c, j, :, mine_in], gs(j), 0)
        arrived(wbuf.at[2, x, c, j, :, mine_in], gs(j), 1)

    def x_send(j):
        ref = wbuf.at[far, x, c, j, :, mine_in]
        for i, d in enumerate(XD):
            send(ref, ref, gs(j), 2 + i, at(dx=d))

    def x_wait(j):
        for i, d in enumerate(XD):
            arrived(wbuf.at[far, (x + 4 - d) % NX, c, j, :, mine_in], gs(j), 2 + i)

    def y_send(j):
        for side, d in ((0, 1), (1, 7)):
            ref = wbuf.at[far, :, c, j, side, mine_in]
            send(ref, ref, gs(j), 5 + side, at(dy=d))

    def y_wait(j):
        for side in (0, 1):
            arrived(wbuf.at[far, :, c, j, side, other_in], gs(j), 5 + side)

    def c_send(j, part):
        ref = wbuf.at[far, :, c, j, :, (mine_in, other_in)[part]]
        send(ref, ref, gs(j), 7 + part, at(dc=1))

    def c_wait(j):
        for part in (0, 1):
            arrived(wbuf.at[far, :, 1 - c, j, :, (mine_in, other_in)[part]], gs(j), 7 + part)

    def xo_send():
        first, second = wbuf.at[0, x, c, direct], wbuf.at[0, x, c, split, :, mine_in]
        for i, d in enumerate(XD):
            send(first, first, qs, i, at(dx=d))
        for i, d in enumerate(XD):
            send(second, second, qs, 3 + i, at(dx=d))

    def xo_wait():
        for i, d in enumerate(XD):
            source = (x + 4 - d) % NX
            arrived(wbuf.at[0, source, c, direct], qs, i)
            arrived(wbuf.at[0, source, c, split, :, mine_in], qs, 3 + i)

    def own_y_send():
        for side, d in ((0, 1), (1, 7)):
            ref = wbuf.at[0, :, c, split, side, mine_in]
            send(ref, ref, qs, 6 + side, at(dy=d))

    def own_y_wait():
        for side in (0, 1):
            arrived(wbuf.at[0, :, c, split, side, other_in], qs, 6 + side)

    def own_part(part, core):
        if part == 0:
            return wbuf.at[0, :, core, direct]
        return wbuf.at[0, :, core, split, :, (mine_in, other_in)[part - 1]]

    def own_c_send(part):
        ref = own_part(part, c)
        send(ref, ref, qs, 8 + part, at(dc=1))

    def own_c_wait():
        for part in (0, 1, 2):
            arrived(own_part(part, 1 - c), qs, 8 + part)

    vs = (vsend, vrecv)

    def v_start():
        src = vbuf.at[0, x, c, :, mine_out]
        send(src, vbuf.at[1, x, c, :, mine_out], vs, 0, at(dz=-4))
        send(src, vbuf.at[2, x, c, :, mine_out], vs, 1, at(dz=4))
        for i, d in enumerate(XD):
            send(src, src, vs, 2 + i, at(dx=d))

    def v_x_send():
        arrived(vbuf.at[1, x, c, :, mine_out], vs, 0)
        arrived(vbuf.at[2, x, c, :, mine_out], vs, 1)
        ref = vbuf.at[far, x, c, :, mine_out]
        for i, d in enumerate(XD):
            send(ref, ref, vs, 5 + i, at(dx=d))

    def v_y_send():
        for i, d in enumerate(XD):
            source = (x + 4 - d) % NX
            arrived(vbuf.at[0, source, c, :, mine_out], vs, 2 + i)
            arrived(vbuf.at[far, source, c, :, mine_out], vs, 5 + i)
        for side, d in ((0, 1), (1, 7)):
            ref = vbuf.at[:, :, c, side, mine_out]
            send(ref, ref, vs, 8 + side, at(dy=d))
        ref = vbuf.at[:, :, c, :, mine_out]
        send(ref, ref, vs, 10, at(dc=1))

    def v_c_send():
        for side in (0, 1):
            arrived(vbuf.at[:, :, c, side, other_out], vs, 8 + side)
        ref = vbuf.at[:, :, c, :, other_out]
        send(ref, ref, vs, 11, at(dc=1))

    def v_wait():
        arrived(vbuf.at[:, :, 1 - c, :, mine_out], vs, 10)
        arrived(vbuf.at[:, :, 1 - c, :, other_out], vs, 11)

    for copy in own_in + own_out:
        copy.wait()
    z_send(0)
    z_send(1)
    xo_send()
    hs = (hsend, hrecv)
    send(frames.at[0, pl.ds(ROWS - EDGE, EDGE)], xbuf.at[pl.ds(0, EDGE)], hs, 0, right)
    send(frames.at[0, pl.ds(0, EDGE)], xbuf.at[pl.ds(EDGE + ROWS, EDGE)], hs, 1, left)

    def norm(start, size):
        values = xbuf[pl.ds(start, size), :].astype(F32)
        centre = jnp.mean(values, axis=-1, keepdims=True)
        deviate = values - centre
        spread = jnp.mean(deviate * deviate, axis=-1, keepdims=True)
        normed = (deviate * lax.rsqrt(spread + 1e-05) * ln_gain[...].reshape(1, D)).astype(BF16)
        for g in range(3):
            nbuf[g, pl.ds(start, size), :] = normed[:, g * 512:(g + 1) * 512]

    own_frames.wait()

    def norm_step(i, carry):
        norm(pl.multiple_of(EDGE + i * 32, 16), 32)
        return carry

    lax.fori_loop(0, ROWS // 32, norm_step, 0)
    arrived(xbuf.at[pl.ds(0, EDGE)], hs, 0)
    norm(0, EDGE)
    arrived(xbuf.at[pl.ds(EDGE + ROWS, EDGE)], hs, 1)
    norm(EDGE + ROWS, EDGE)

    def dot(g, j, m, size):
        w = [wbuf[g, :, :, j, side].reshape(512, 128) for side in (0, 1)]
        rows = nbuf[(zh + g) % 3, pl.ds(m, size), :]
        return jnp.dot(rows, jnp.concatenate(w, axis=1), preferred_element_type=F32)

    def first_dot(j, carry):
        acc[j] = dot(0, j, 0, ALL)
        return carry

    length = lengths[0]
    HM = ALL // 2

    def gate_step(j):
        def half(m, carry):
            m0 = pl.multiple_of(m * HM, 16)
            position = t * ROWS - EDGE + m0 + lax.broadcasted_iota(jnp.int32, (HM, 128), 0)
            valid = (position >= 0) & (position < length)
            pair = acc[j, pl.ds(m0, HM), :] + (dot(1, j, m0, HM) + dot(2, j, m0, HM))
            gated = jnp.where(valid, pair[:, :128] * sigmoid(pair[:, 128:]), 0.0)
            gbuf[j, pl.ds(m0, HM), :] = gated.astype(BF16).astype(F32)
            return carry

        lax.fori_loop(0, 2, half, 0)

    local = jnp.clip(length - t * ROWS, 0, ROWS).astype(F32)
    BLOCK = 64

    def conv_step(s):
        lanes = pl.ds(pl.multiple_of(s * 128, 128), 128)
        total = jnp.zeros((8, 128), F32)
        for b in range(0, ROWS, BLOCK):
            value = jnp.zeros((BLOCK, 128), F32)
            for k in range(TAPS):
                value = value + gbuf[s, pl.ds(b + 1 + k, BLOCK), :] * dw[pl.ds(k, 1), lanes]
            cbuf[s, pl.ds(b, BLOCK), :] = value
            position = t * ROWS + b + lax.broadcasted_iota(jnp.int32, (BLOCK, 128), 0)
            masked = jnp.where(position < length, value, 0.0)
            total = total + masked.reshape(BLOCK // 8, 8, 128).sum(axis=0)
        mean = total.sum(axis=0, keepdims=True) / jnp.maximum(local, 1.0)
        square = jnp.zeros((8, 128), F32)
        for b in range(0, ROWS, BLOCK):
            position = t * ROWS + b + lax.broadcasted_iota(jnp.int32, (BLOCK, 128), 0)
            delta = jnp.where(position < length, cbuf[s, pl.ds(b, BLOCK), :] - mean, 0.0)
            square = square + (delta * delta).reshape(BLOCK // 8, 8, 128).sum(axis=0)
        pay[s // 3, pl.ds(s % 3, 1), :] = mean
        pay[s // 3, pl.ds(s % 3 + 4, 1), :] = square.sum(axis=0, keepdims=True)
        pltpu.make_async_copy(cbuf.at[s], conv.at[s], csem.at[s]).start()

    pay[...] = jnp.zeros((2, 8, 128), F32)
    for side in (0, 1):
        pay[side, 3:4, :] = jnp.full((1, 128), local, F32)

    X_LAG, Y_LAG, C_LAG = 3, 6, 7

    def pipeline(i, carry):
        @pl.when(i < STRIPS)
        def _():
            z_wait(i)
            x_send(i)

        @pl.when(i < STRIPS - 2)
        def _():
            z_send(i + 2)

        @pl.when((i >= X_LAG) & (i < STRIPS + X_LAG))
        def _():
            x_wait(i - X_LAG)
            y_send(i - X_LAG)
            c_send(i - X_LAG, 0)

        @pl.when(i == 2)
        def _():
            xo_wait()
            own_y_send()
            own_c_send(0)
            own_c_send(1)

        @pl.when(i == 5)
        def _():
            v_start()

        @pl.when(i == 6)
        def _():
            own_y_wait()
            own_c_send(2)

        @pl.when((i >= Y_LAG) & (i < STRIPS + Y_LAG))
        def _():
            y_wait(i - Y_LAG)
            c_send(i - Y_LAG, 1)

        @pl.when(i == 7)
        def _():
            own_c_wait()
            lax.fori_loop(0, STRIPS, first_dot, 0)

        @pl.when(i == 9)
        def _():
            v_x_send()

        @pl.when(i >= C_LAG)
        def _():
            j = i - C_LAG
            c_wait(j)
            gate_step(j)
            conv_step(j)

        return carry

    lax.fori_loop(0, STRIPS + C_LAG, pipeline, 0)
    v_y_send()

    def drain(j, carry):
        src = wbuf.at[0, x, c, j, :, mine_in]
        for k in (0, 1):
            remote(src, src, gs(j), k, at(dc=1)).wait_send()
        for k in (2, 3, 4):
            ref = wbuf.at[far, x, c, j, :, mine_in]
            remote(ref, ref, gs(j), k, at(dc=1)).wait_send()
        for side in (0, 1):
            ref = wbuf.at[far, :, c, j, side, mine_in]
            remote(ref, ref, gs(j), 5 + side, at(dc=1)).wait_send()
        for part in (0, 1):
            ref = wbuf.at[far, :, c, j, :, (mine_in, other_in)[part]]
            remote(ref, ref, gs(j), 7 + part, at(dc=1)).wait_send()
        return carry

    leaving = [(wbuf.at[0, x, c, direct], qs, k) for k in (0, 1, 2)]
    leaving += [(wbuf.at[0, x, c, split, :, mine_in], qs, k) for k in (3, 4, 5)]
    leaving += [(wbuf.at[0, :, c, split, side, mine_in], qs, 6 + side) for side in (0, 1)]
    leaving += [(own_part(part, c), qs, 8 + part) for part in (0, 1, 2)]
    later = [(vbuf.at[0, x, c, :, mine_out], vs, k) for k in range(5)]
    later += [(vbuf.at[far, x, c, :, mine_out], vs, k) for k in (5, 6, 7)]
    later += [(vbuf.at[:, :, c, side, mine_out], vs, 8 + side) for side in (0, 1)]
    later += [(vbuf.at[:, :, c, :, rows], vs, 10 + k) for k, rows in enumerate((mine_out, other_out))]

    def settle(items):
        for ref, sems, k in items:
            remote(ref, ref, sems, k, at(dc=1)).wait_send()

    def after_z():
        v_c_send()
        lax.fori_loop(0, STRIPS, drain, 0)
        settle(leaving)

    wide_copy = pltpu.make_async_copy(vbuf, wide, csem.at[STRIPS])

    def after_y():
        v_wait()
        wide_copy.start()
        settle(later)

    def exchange(ref, slot, count, base, to, source=None, between=None):
        sems = (ssend, srecv)
        for d in range(1, count):
            src = ref.at[slot] if source is None else source(d)
            send(src, ref.at[slot], sems, base + d, to(d))
        if between is not None:
            between()
        for d in range(1, count):
            arrived(ref.at[(slot + count - d) % count], sems, base + d)
        return combine(ref, count)

    r1[slot1] = pay[c]
    r2[z] = exchange(r1, slot1, 8, 0, peer1, lambda d: pay.at[(slot1 + d) % 2])
    r3[y] = exchange(r2, z, NZ, 8, lambda d: at(dz=d), None, after_z)
    final[c] = exchange(r3, y, NY, 20, lambda d: at(dy=d), None, after_y)
    send(final.at[c], final.at[c], (ssend, srecv), 0, at(dc=1))
    for args in sent[:-1]:
        remote(*args).wait_send()
    for s in range(STRIPS):
        pltpu.make_async_copy(cbuf.at[s], conv.at[s], csem.at[s]).wait()
    wide_copy.wait()
    arrived(final.at[1 - c], (ssend, srecv), 0)
    stats[...] = final[...]
    remote(*sent[-1]).wait_send()


TM = 128


def finish(lengths, stats, bn_gain, bn_shift, conv, wide, out, act):
    zh, t = lax.axis_index("fsdp") // (2 * NX), lax.axis_index("ctx")
    for s in range(STRIPS):
        lanes = slice(s * 128, (s + 1) * 128)
        side, row = s // 3, s % 3
        count = stats[side, 3:4, :]
        spread = stats[side, 4 + row:5 + row, :] / count
        factor = lax.rsqrt(spread + 1e-05) * bn_gain[lanes].reshape(1, 128)
        value = (conv[s] - stats[side, row:row + 1, :]) * factor + bn_shift[lanes].reshape(1, 128)
        act[s // 2, :, (s % 2) * 128:(s % 2 + 1) * 128] = (value * sigmoid(value)).astype(BF16)
    start = t * ROWS + pl.program_id(0) * TM
    valid = start + lax.broadcasted_iota(jnp.int32, (TM, CH), 0) < lengths[0]
    for side in (0, 1):
        res = 0.0
        for g in range(3):
            w = wide[g, :, :, side].reshape(256, CH)
            res = res + jnp.dot(act[(zh + g) % 3], w, preferred_element_type=F32)
        out[0, :, side * CH:(side + 1) * CH] = jnp.where(valid, res, 0.0).astype(BF16)


def body(frames, lengths, ln_gain, w_in, dw_kernel, bn_gain, bn_shift, w_out):
    hbm = pl.BlockSpec(memory_space=pltpu.HBM)
    vmem = pl.BlockSpec(memory_space=pltpu.VMEM)
    smem = pl.BlockSpec(memory_space=pltpu.SMEM)
    wide_shape = (3, NX, 2, 2, 32, CH)
    conv, wide, stats = pl.pallas_call(
        kernel,
        out_shape=(
            jax.ShapeDtypeStruct((STRIPS, ROWS, 128), F32),
            jax.ShapeDtypeStruct(wide_shape, BF16),
            jax.ShapeDtypeStruct((2, 8, 128), F32),
        ),
        in_specs=[hbm, smem, vmem, hbm, vmem, hbm],
        out_specs=(hbm, hbm, vmem),
        scratch_shapes=[
            pltpu.VMEM((ALL, D), BF16),
            pltpu.VMEM((3, ALL, 512), BF16),
            pltpu.VMEM((3, NX, 2, STRIPS, 2, 64, 128), BF16),
            pltpu.VMEM((3, NX, 2, 2, 32, CH), BF16),
            pltpu.VMEM((6, ALL, 256), F32),
            pltpu.VMEM((STRIPS, ALL, 128), F32),
            pltpu.VMEM((STRIPS, ROWS, 128), F32),
            pltpu.VMEM((2, 8, 128), F32),
            pltpu.VMEM((8, 8, 128), F32),
            pltpu.VMEM((NZ, 8, 128), F32),
            pltpu.VMEM((NY, 8, 128), F32),
            pltpu.VMEM((2, 8, 128), F32),
            pltpu.SemaphoreType.DMA((STRIPS, 9)),
            pltpu.SemaphoreType.DMA((STRIPS, 9)),
            pltpu.SemaphoreType.DMA((11,)),
            pltpu.SemaphoreType.DMA((11,)),
            pltpu.SemaphoreType.DMA((12,)),
            pltpu.SemaphoreType.DMA((12,)),
            pltpu.SemaphoreType.DMA((2,)),
            pltpu.SemaphoreType.DMA((2,)),
            pltpu.SemaphoreType.DMA((28,)),
            pltpu.SemaphoreType.DMA((28,)),
            pltpu.SemaphoreType.DMA((15,)),
            pltpu.SemaphoreType.DMA((STRIPS + 1,)),
        ],
        compiler_params=pltpu.CompilerParams(
            collective_id=0, has_side_effects=True, vmem_limit_bytes=63 << 20
        ),
        name="conformer_conv",
    )(frames, lengths, ln_gain, w_in, dw_kernel, w_out)
    return pl.pallas_call(
        finish,
        out_shape=jax.ShapeDtypeStruct((1, ROWS, D), BF16),
        grid=(ROWS // TM,),
        in_specs=[
            smem, vmem, vmem, vmem,
            pl.BlockSpec((STRIPS, TM, 128), lambda i: (0, i, 0)),
            pl.BlockSpec(wide_shape, lambda i: (0,) * 6, pipeline_mode=pl.Buffered(1)),
        ],
        out_specs=pl.BlockSpec((1, TM, D), lambda i: (0, i, 0)),
        scratch_shapes=[pltpu.VMEM((3, TM, 256), BF16)],
        compiler_params=pltpu.CompilerParams(vmem_limit_bytes=63 << 20),
        name="finish",
    )(lengths, stats, bn_gain, bn_shift, conv, wide)


def solution(mesh):
    return jax.shard_map(
        body,
        mesh=mesh,
        in_specs=(
            P("fsdp", "ctx", None),
            P("fsdp"),
            P(),
            P("fsdp", None),
            P(),
            P(),
            P(),
            P("fsdp", None),
        ),
        out_specs=P("fsdp", "ctx", None),
        check_vma=False,
    )
```

```python
import jax
import jax.numpy as jnp
from jax import lax
from jax.experimental import pallas as pl
from jax.experimental.pallas import tpu as pltpu
from jax.sharding import PartitionSpec as P

MESH = pl.DeviceIdType.MESH
BF16 = jnp.bfloat16
F32 = jnp.float32
NX, NY, NZ = 4, 8, 12
ROWS, EDGE = 512, 16
ALL = ROWS + 2 * EDGE
TAPS, CH, D = 31, 768, 1536
STRIPS = CH // 128
AHEAD = 4


def device_of(x, y, z, c):
    return (((z // 4) * NX + x) * 2 + c, (z % 4) * NY + y)


def sigmoid(v):
    return 0.5 * jnp.tanh(0.5 * v) + 0.5


def combine(all_ref, parts):
    tables = [all_ref[i] for i in range(parts)]
    counts = [all_ref[i, 3:4, :] for i in range(parts)]
    total = sum(counts[1:], counts[0])
    weighted = [m * n for m, n in zip(tables, counts)]
    mean = sum(weighted[1:], weighted[0]) / jnp.maximum(total, 1.0)
    added = [n * (m - mean) * (m - mean) for m, n in zip(tables, counts)]
    square = sum(tables[1:], tables[0]) + pltpu.roll(sum(added[1:], added[0]), 4, 0)
    row = lax.broadcasted_iota(jnp.int32, (8, 128), 0)
    rest = jnp.where(row == 7, 0.0, square)
    return jnp.where(row < 3, mean, jnp.where(row == 3, jnp.broadcast_to(total, (8, 128)), rest))


def kernel(
    frames, lengths, ln_gain, w_in, dw, w_out, conv, wide, stats,
    xbuf, nbuf, wbuf, vbuf, gbuf, cbuf, pay, r1, r2, r3, final,
    gsend, grecv, qsend, qrecv, vsend, vrecv, hsend, hrecv, ssend, srecv, lsem, csem,
):
    f, t = lax.axis_index("fsdp"), lax.axis_index("ctx")
    x, c = (f // 2) % NX, f % 2
    y = t % NY
    zh, zl = f // (2 * NX), t // NY
    z = zh * 4 + zl
    par = y % 2
    up, down = (zh + 1) % 3, (zh + 2) % 3
    groups = (zh, up, down)

    def at(dx=0, dy=0, dz=0, dc=0):
        return device_of((x + dx) % NX, (y + dy) % NY, (z + dz) % NZ, (c + dc) % 2)

    left, right = (f, (t + 31) % 32), (f, (t + 1) % 32)
    slot1 = x * 2 + c

    def peer1(d):
        to = (slot1 + d) % 8
        return device_of(to // 2, y, z, to % 2)

    peers = [left, right]
    peers += [peer1(d) for d in range(1, 8)]
    peers += [at(dy=d) for d in range(1, NY)]
    peers += [at(dz=d) for d in range(1, NZ)]

    mine_in = pl.ds(pl.multiple_of(par * 32, 32), 32)
    other_in = pl.ds(pl.multiple_of((1 - par) * 32, 32), 32)
    mine_out = pl.ds(pl.multiple_of(par * 16, 16), 16)
    other_out = pl.ds(pl.multiple_of((1 - par) * 16, 16), 16)
    direct, split = pl.ds(0, 3), pl.ds(3, 3)
    far = pl.ds(1, 2)

    own_frames = pltpu.make_async_copy(frames.at[0], xbuf.at[pl.ds(EDGE, ROWS)], lsem.at[0])
    own_frames.start()
    own_in, own_out = [], []
    for j in range(STRIPS):
        for side in (0, 1):
            cols = pl.ds(side * CH + j * 128, 128)
            src, dst = w_in.at[:, cols], wbuf.at[0, x, c, j, side]
            if j >= 3:
                src, dst = w_in.at[mine_in, cols], wbuf.at[0, x, c, j, side, mine_in]
            own_in.append(pltpu.make_async_copy(src, dst, lsem.at[1 + len(own_in)]))
    for side in (0, 1):
        src = w_out.at[mine_out, pl.ds(side * CH, CH)]
        own_out.append(pltpu.make_async_copy(src, vbuf.at[0, x, c, side, mine_out], lsem.at[13 + side]))
    for copy in own_in + own_out:
        copy.start()

    barrier = pltpu.get_barrier_semaphore()
    for peer in peers:
        pl.semaphore_signal(barrier, inc=1, device_id=peer, device_id_type=MESH)
    pl.semaphore_wait(barrier, len(peers))

    sent = []

    def remote(src, dst, sems, k, to):
        return pltpu.make_async_remote_copy(
            src_ref=src, dst_ref=dst, send_sem=sems[0].at[k], recv_sem=sems[1].at[k],
            device_id=to, device_id_type=MESH,
        )

    def send(*args):
        remote(*args).start()
        if args[2][0] is hsend or args[2][0] is ssend:
            sent.append(args)

    def arrived(dst, sems, k):
        remote(dst, dst, sems, k, at(dc=1)).wait_recv()

    XD = (1, 3, 2)

    def gs(j):
        return (gsend.at[j], grecv.at[j])

    qs = (qsend, qrecv)

    def z_send(j):
        src = wbuf.at[0, x, c, j, :, mine_in]
        send(src, wbuf.at[1, x, c, j, :, mine_in], gs(j), 0, at(dz=-4))
        send(src, wbuf.at[2, x, c, j, :, mine_in], gs(j), 1, at(dz=4))

    def z_wait(j):
        arrived(wbuf.at[1, x, c, j, :, mine_in], gs(j), 0)
        arrived(wbuf.at[2, x, c, j, :, mine_in], gs(j), 1)

    def x_send(j):
        ref = wbuf.at[far, x, c, j, :, mine_in]
        for i, d in enumerate(XD):
            send(ref, ref, gs(j), 2 + i, at(dx=d))

    def x_wait(j):
        for i, d in enumerate(XD):
            arrived(wbuf.at[far, (x + 4 - d) % NX, c, j, :, mine_in], gs(j), 2 + i)

    def y_send(j):
        for side, d in ((0, 1), (1, 7)):
            ref = wbuf.at[far, :, c, j, side, mine_in]
            send(ref, ref, gs(j), 5 + side, at(dy=d))

    def y_wait(j):
        for side in (0, 1):
            arrived(wbuf.at[far, :, c, j, side, other_in], gs(j), 5 + side)

    def c_send(j, part):
        ref = wbuf.at[far, :, c, j, :, (mine_in, other_in)[part]]
        send(ref, ref, gs(j), 7 + part, at(dc=1))

    def c_wait(j):
        for part in (0, 1):
            arrived(wbuf.at[far, :, 1 - c, j, :, (mine_in, other_in)[part]], gs(j), 7 + part)

    def xo_send():
        first, second = wbuf.at[0, x, c, direct], wbuf.at[0, x, c, split, :, mine_in]
        for i, d in enumerate(XD):
            send(first, first, qs, i, at(dx=d))
        for i, d in enumerate(XD):
            send(second, second, qs, 3 + i, at(dx=d))

    def xo_wait():
        for i, d in enumerate(XD):
            source = (x + 4 - d) % NX
            arrived(wbuf.at[0, source, c, direct], qs, i)
            arrived(wbuf.at[0, source, c, split, :, mine_in], qs, 3 + i)

    def own_y_send():
        for side, d in ((0, 1), (1, 7)):
            ref = wbuf.at[0, :, c, split, side, mine_in]
            send(ref, ref, qs, 6 + side, at(dy=d))

    def own_y_wait():
        for side in (0, 1):
            arrived(wbuf.at[0, :, c, split, side, other_in], qs, 6 + side)

    def own_part(part, core):
        if part == 0:
            return wbuf.at[0, :, core, direct]
        return wbuf.at[0, :, core, split, :, (mine_in, other_in)[part - 1]]

    def own_c_send(part):
        ref = own_part(part, c)
        send(ref, ref, qs, 8 + part, at(dc=1))

    def own_c_wait():
        for part in (0, 1, 2):
            arrived(own_part(part, 1 - c), qs, 8 + part)

    vs = (vsend, vrecv)

    def v_start():
        src = vbuf.at[0, x, c, :, mine_out]
        send(src, vbuf.at[1, x, c, :, mine_out], vs, 0, at(dz=-4))
        send(src, vbuf.at[2, x, c, :, mine_out], vs, 1, at(dz=4))
        for i, d in enumerate(XD):
            send(src, src, vs, 2 + i, at(dx=d))

    def v_x_send():
        arrived(vbuf.at[1, x, c, :, mine_out], vs, 0)
        arrived(vbuf.at[2, x, c, :, mine_out], vs, 1)
        ref = vbuf.at[far, x, c, :, mine_out]
        for i, d in enumerate(XD):
            send(ref, ref, vs, 5 + i, at(dx=d))

    def v_y_send():
        for i, d in enumerate(XD):
            source = (x + 4 - d) % NX
            arrived(vbuf.at[0, source, c, :, mine_out], vs, 2 + i)
            arrived(vbuf.at[far, source, c, :, mine_out], vs, 5 + i)
        for side, d in ((0, 1), (1, 7)):
            ref = vbuf.at[:, :, c, side, mine_out]
            send(ref, ref, vs, 8 + side, at(dy=d))
        ref = vbuf.at[:, :, c, :, mine_out]
        send(ref, ref, vs, 10, at(dc=1))

    def v_c_send():
        for side in (0, 1):
            arrived(vbuf.at[:, :, c, side, other_out], vs, 8 + side)
        ref = vbuf.at[:, :, c, :, other_out]
        send(ref, ref, vs, 11, at(dc=1))

    def v_wait():
        arrived(vbuf.at[:, :, 1 - c, :, mine_out], vs, 10)
        arrived(vbuf.at[:, :, 1 - c, :, other_out], vs, 11)

    for copy in own_in + own_out:
        copy.wait()
    for j in range(AHEAD):
        z_send(j)
    xo_send()
    hs = (hsend, hrecv)
    send(frames.at[0, pl.ds(ROWS - EDGE, EDGE)], xbuf.at[pl.ds(0, EDGE)], hs, 0, right)
    send(frames.at[0, pl.ds(0, EDGE)], xbuf.at[pl.ds(EDGE + ROWS, EDGE)], hs, 1, left)

    def norm(start, size):
        values = xbuf[pl.ds(start, size), :].astype(F32)
        centre = jnp.mean(values, axis=-1, keepdims=True)
        deviate = values - centre
        spread = jnp.mean(deviate * deviate, axis=-1, keepdims=True)
        normed = (deviate * lax.rsqrt(spread + 1e-05) * ln_gain[...].reshape(1, D)).astype(BF16)
        for g in range(3):
            nbuf[g, pl.ds(start, size), :] = normed[:, g * 512:(g + 1) * 512]

    own_frames.wait()

    def norm_step(i, carry):
        norm(pl.multiple_of(EDGE + i * 32, 16), 32)
        return carry

    lax.fori_loop(0, ROWS // 32, norm_step, 0)
    arrived(xbuf.at[pl.ds(0, EDGE)], hs, 0)
    norm(0, EDGE)
    arrived(xbuf.at[pl.ds(EDGE + ROWS, EDGE)], hs, 1)
    norm(EDGE + ROWS, EDGE)

    def dot(g, j, m, size):
        w = [wbuf[g, :, :, j, side].reshape(512, 128) for side in (0, 1)]
        rows = nbuf[(zh + g) % 3, pl.ds(m, size), :]
        return jnp.dot(rows, jnp.concatenate(w, axis=1), preferred_element_type=F32)

    length = lengths[0]
    HM = ALL // 2

    def gate_step(j):
        def half(m, carry):
            m0 = pl.multiple_of(m * HM, 16)
            position = t * ROWS - EDGE + m0 + lax.broadcasted_iota(jnp.int32, (HM, 128), 0)
            valid = (position >= 0) & (position < length)
            pair = dot(0, j, m0, HM) + dot(1, j, m0, HM) + dot(2, j, m0, HM)
            gated = jnp.where(valid, pair[:, :128] * sigmoid(pair[:, 128:]), 0.0)
            gbuf[j, pl.ds(m0, HM), :] = gated.astype(BF16).astype(F32)
            return carry

        lax.fori_loop(0, 2, half, 0)

    local = jnp.clip(length - t * ROWS, 0, ROWS).astype(F32)
    BLOCK = 64

    def conv_step(s):
        lanes = pl.ds(pl.multiple_of(s * 128, 128), 128)
        total = jnp.zeros((8, 128), F32)
        for b in range(0, ROWS, BLOCK):
            value = jnp.zeros((BLOCK, 128), F32)
            for k in range(TAPS):
                value = value + gbuf[s, pl.ds(b + 1 + k, BLOCK), :] * dw[pl.ds(k, 1), lanes]
            cbuf[s, pl.ds(b, BLOCK), :] = value
            position = t * ROWS + b + lax.broadcasted_iota(jnp.int32, (BLOCK, 128), 0)
            masked = jnp.where(position < length, value, 0.0)
            total = total + masked.reshape(BLOCK // 8, 8, 128).sum(axis=0)
        mean = total.sum(axis=0, keepdims=True) / jnp.maximum(local, 1.0)
        square = jnp.zeros((8, 128), F32)
        for b in range(0, ROWS, BLOCK):
            position = t * ROWS + b + lax.broadcasted_iota(jnp.int32, (BLOCK, 128), 0)
            delta = jnp.where(position < length, cbuf[s, pl.ds(b, BLOCK), :] - mean, 0.0)
            square = square + (delta * delta).reshape(BLOCK // 8, 8, 128).sum(axis=0)
        pay[s // 3, pl.ds(s % 3, 1), :] = mean
        pay[s // 3, pl.ds(s % 3 + 4, 1), :] = square.sum(axis=0, keepdims=True)
        pltpu.make_async_copy(cbuf.at[s], conv.at[s], csem.at[s]).start()

    pay[...] = jnp.zeros((2, 8, 128), F32)
    for side in (0, 1):
        pay[side, 3:4, :] = jnp.full((1, 128), local, F32)

    X_LAG, Y_LAG, C_LAG = 3, 6, 7

    def pipeline(i, carry):
        @pl.when(i < STRIPS)
        def _():
            z_wait(i)
            x_send(i)

        @pl.when(i < STRIPS - AHEAD)
        def _():
            z_send(jnp.minimum(i + AHEAD, STRIPS - 1))

        @pl.when((i >= X_LAG) & (i < STRIPS + X_LAG))
        def _():
            x_wait(i - X_LAG)
            y_send(i - X_LAG)
            c_send(i - X_LAG, 0)

        @pl.when(i == 2)
        def _():
            xo_wait()
            own_y_send()
            own_c_send(0)
            own_c_send(1)

        @pl.when(i == 5)
        def _():
            v_start()

        @pl.when(i == 6)
        def _():
            own_y_wait()
            own_c_send(2)

        @pl.when((i >= Y_LAG) & (i < STRIPS + Y_LAG))
        def _():
            y_wait(i - Y_LAG)
            c_send(i - Y_LAG, 1)

        @pl.when(i == 7)
        def _():
            own_c_wait()

        @pl.when(i == 9)
        def _():
            v_x_send()

        @pl.when(i >= C_LAG)
        def _():
            j = i - C_LAG
            c_wait(j)
            gate_step(j)
            conv_step(j)

        return carry

    lax.fori_loop(0, STRIPS + C_LAG, pipeline, 0)
    v_y_send()

    def drain(j, carry):
        src = wbuf.at[0, x, c, j, :, mine_in]
        for k in (0, 1):
            remote(src, src, gs(j), k, at(dc=1)).wait_send()
        for k in (2, 3, 4):
            ref = wbuf.at[far, x, c, j, :, mine_in]
            remote(ref, ref, gs(j), k, at(dc=1)).wait_send()
        for side in (0, 1):
            ref = wbuf.at[far, :, c, j, side, mine_in]
            remote(ref, ref, gs(j), 5 + side, at(dc=1)).wait_send()
        for part in (0, 1):
            ref = wbuf.at[far, :, c, j, :, (mine_in, other_in)[part]]
            remote(ref, ref, gs(j), 7 + part, at(dc=1)).wait_send()
        return carry

    leaving = [(wbuf.at[0, x, c, direct], qs, k) for k in (0, 1, 2)]
    leaving += [(wbuf.at[0, x, c, split, :, mine_in], qs, k) for k in (3, 4, 5)]
    leaving += [(wbuf.at[0, :, c, split, side, mine_in], qs, 6 + side) for side in (0, 1)]
    leaving += [(own_part(part, c), qs, 8 + part) for part in (0, 1, 2)]
    later = [(vbuf.at[0, x, c, :, mine_out], vs, k) for k in range(5)]
    later += [(vbuf.at[far, x, c, :, mine_out], vs, k) for k in (5, 6, 7)]
    later += [(vbuf.at[:, :, c, side, mine_out], vs, 8 + side) for side in (0, 1)]
    later += [(vbuf.at[:, :, c, :, rows], vs, 10 + k) for k, rows in enumerate((mine_out, other_out))]

    def settle(items):
        for ref, sems, k in items:
            remote(ref, ref, sems, k, at(dc=1)).wait_send()

    def after_z():
        v_c_send()
        lax.fori_loop(0, STRIPS, drain, 0)
        settle(leaving)

    wide_copies = [
        pltpu.make_async_copy(vbuf.at[g], wide.at[(zh + g) % 3], csem.at[STRIPS + g]) for g in range(3)
    ]

    def after_y():
        v_wait()
        for copy in wide_copies:
            copy.start()
        settle(later)

    def exchange(ref, slot, count, base, to, source=None, between=None):
        sems = (ssend, srecv)
        for d in range(1, count):
            src = ref.at[slot] if source is None else source(d)
            send(src, ref.at[slot], sems, base + d, to(d))
        if between is not None:
            between()
        for d in range(1, count):
            arrived(ref.at[(slot + count - d) % count], sems, base + d)
        return combine(ref, count)

    r1[slot1] = pay[c]
    r2[z] = exchange(r1, slot1, 8, 0, peer1, lambda d: pay.at[(slot1 + d) % 2])
    r3[y] = exchange(r2, z, NZ, 8, lambda d: at(dz=d), None, after_z)
    final[c] = exchange(r3, y, NY, 20, lambda d: at(dy=d), None, after_y)
    send(final.at[c], final.at[c], (ssend, srecv), 0, at(dc=1))
    for args in sent[:-1]:
        remote(*args).wait_send()
    for s in range(STRIPS):
        pltpu.make_async_copy(cbuf.at[s], conv.at[s], csem.at[s]).wait()
    for copy in wide_copies:
        copy.wait()
    arrived(final.at[1 - c], (ssend, srecv), 0)
    stats[...] = final[...]
    remote(*sent[-1]).wait_send()


TM = 256


def finish(lengths, stats, bn_gain, bn_shift, conv, wide, out, act):
    t, i = lax.axis_index("ctx"), pl.program_id(0)
    for s in range(STRIPS):
        lanes = slice(s * 128, (s + 1) * 128)
        side, row = s // 3, s % 3
        count = stats[side, 3:4, :]
        spread = stats[side, 4 + row:5 + row, :] / count
        factor = lax.rsqrt(spread + 1e-05) * bn_gain[lanes].reshape(1, 128)
        value = (conv[s] - stats[side, row:row + 1, :]) * factor + bn_shift[lanes].reshape(1, 128)
        act[:, lanes] = (value * sigmoid(value)).astype(BF16)
    start = t * ROWS + i * TM
    valid = start + lax.broadcasted_iota(jnp.int32, (TM, CH), 0) < lengths[0]
    for side in (0, 1):
        w = wide[:, :, :, side].reshape(CH, CH)
        res = jnp.dot(act[...], w, preferred_element_type=F32)
        out[0, :, side * CH:(side + 1) * CH] = jnp.where(valid, res, 0.0).astype(BF16)


def body(frames, lengths, ln_gain, w_in, dw_kernel, bn_gain, bn_shift, w_out):
    hbm = pl.BlockSpec(memory_space=pltpu.HBM)
    vmem = pl.BlockSpec(memory_space=pltpu.VMEM)
    smem = pl.BlockSpec(memory_space=pltpu.SMEM)
    wide_shape = (3, NX, 2, 2, 32, CH)
    conv, wide, stats = pl.pallas_call(
        kernel,
        out_shape=(
            jax.ShapeDtypeStruct((STRIPS, ROWS, 128), F32),
            jax.ShapeDtypeStruct(wide_shape, BF16),
            jax.ShapeDtypeStruct((2, 8, 128), F32),
        ),
        in_specs=[hbm, smem, vmem, hbm, vmem, hbm],
        out_specs=(hbm, hbm, vmem),
        scratch_shapes=[
            pltpu.VMEM((ALL, D), BF16),
            pltpu.VMEM((3, ALL, 512), BF16),
            pltpu.VMEM((3, NX, 2, STRIPS, 2, 64, 128), BF16),
            pltpu.VMEM((3, NX, 2, 2, 32, CH), BF16),
            pltpu.VMEM((STRIPS, ALL, 128), F32),
            pltpu.VMEM((STRIPS, ROWS, 128), F32),
            pltpu.VMEM((2, 8, 128), F32),
            pltpu.VMEM((8, 8, 128), F32),
            pltpu.VMEM((NZ, 8, 128), F32),
            pltpu.VMEM((NY, 8, 128), F32),
            pltpu.VMEM((2, 8, 128), F32),
            pltpu.SemaphoreType.DMA((STRIPS, 9)),
            pltpu.SemaphoreType.DMA((STRIPS, 9)),
            pltpu.SemaphoreType.DMA((11,)),
            pltpu.SemaphoreType.DMA((11,)),
            pltpu.SemaphoreType.DMA((12,)),
            pltpu.SemaphoreType.DMA((12,)),
            pltpu.SemaphoreType.DMA((2,)),
            pltpu.SemaphoreType.DMA((2,)),
            pltpu.SemaphoreType.DMA((28,)),
            pltpu.SemaphoreType.DMA((28,)),
            pltpu.SemaphoreType.DMA((15,)),
            pltpu.SemaphoreType.DMA((STRIPS + 3,)),
        ],
        compiler_params=pltpu.CompilerParams(
            collective_id=0, has_side_effects=True, vmem_limit_bytes=63 << 20
        ),
        name="conformer_conv",
    )(frames, lengths, ln_gain, w_in, dw_kernel, w_out)
    return pl.pallas_call(
        finish,
        out_shape=jax.ShapeDtypeStruct((1, ROWS, D), BF16),
        grid=(ROWS // TM,),
        in_specs=[
            smem, vmem, vmem, vmem,
            pl.BlockSpec((STRIPS, TM, 128), lambda i: (0, i, 0)),
            pl.BlockSpec(wide_shape, lambda i: (0,) * 6, pipeline_mode=pl.Buffered(1)),
        ],
        out_specs=pl.BlockSpec((1, TM, D), lambda i: (0, i, 0)),
        scratch_shapes=[pltpu.VMEM((TM, CH), BF16)],
        compiler_params=pltpu.CompilerParams(vmem_limit_bytes=63 << 20),
        name="finish",
    )(lengths, stats, bn_gain, bn_shift, conv, wide)


def solution(mesh):
    return jax.shard_map(
        body,
        mesh=mesh,
        in_specs=(
            P("fsdp", "ctx", None),
            P("fsdp"),
            P(),
            P("fsdp", None),
            P(),
            P(),
            P(),
            P("fsdp", None),
        ),
        out_specs=P("fsdp", "ctx", None),
        check_vma=False,
    )
```

```python
import jax
import jax.numpy as jnp
from jax import lax
from jax.experimental import pallas as pl
from jax.experimental.pallas import tpu as pltpu
from jax.sharding import PartitionSpec as P

MESH = pl.DeviceIdType.MESH
BF16 = jnp.bfloat16
F32 = jnp.float32
NX, NY, NZ = 4, 8, 12
ROWS, EDGE = 512, 16
ALL = ROWS + 2 * EDGE
TAPS, CH, D = 31, 768, 1536
STRIPS = CH // 128
AHEAD = 4


def device_of(x, y, z, c):
    return (((z // 4) * NX + x) * 2 + c, (z % 4) * NY + y)


def sigmoid(v):
    return 0.5 * jnp.tanh(0.5 * v) + 0.5


def combine(all_ref, parts):
    tables = [all_ref[i] for i in range(parts)]
    counts = [all_ref[i, 3:4, :] for i in range(parts)]
    total = sum(counts[1:], counts[0])
    weighted = [m * n for m, n in zip(tables, counts)]
    mean = sum(weighted[1:], weighted[0]) / jnp.maximum(total, 1.0)
    added = [n * (m - mean) * (m - mean) for m, n in zip(tables, counts)]
    square = sum(tables[1:], tables[0]) + pltpu.roll(sum(added[1:], added[0]), 4, 0)
    row = lax.broadcasted_iota(jnp.int32, (8, 128), 0)
    rest = jnp.where(row == 7, 0.0, square)
    return jnp.where(row < 3, mean, jnp.where(row == 3, jnp.broadcast_to(total, (8, 128)), rest))


def kernel(
    frames, lengths, ln_gain, w_in, dw, w_out, conv, wide, stats,
    xbuf, nbuf, wbuf, vbuf, gbuf, cbuf, pay, r1, r2, r3, final,
    gsend, grecv, qsend, qrecv, vsend, vrecv, hsend, hrecv, ssend, srecv, lsem, csem,
):
    f, t = lax.axis_index("fsdp"), lax.axis_index("ctx")
    x, c = (f // 2) % NX, f % 2
    y = t % NY
    zh, zl = f // (2 * NX), t // NY
    z = zh * 4 + zl
    par = y % 2
    up, down = (zh + 1) % 3, (zh + 2) % 3
    groups = (zh, up, down)

    def at(dx=0, dy=0, dz=0, dc=0):
        return device_of((x + dx) % NX, (y + dy) % NY, (z + dz) % NZ, (c + dc) % 2)

    left, right = (f, (t + 31) % 32), (f, (t + 1) % 32)
    slot1 = x * 2 + c

    def peer1(d):
        to = (slot1 + d) % 8
        return device_of(to // 2, y, z, to % 2)

    peers = [left, right]
    peers += [peer1(d) for d in range(1, 8)]
    peers += [at(dy=d) for d in range(1, NY)]
    peers += [at(dz=d) for d in range(1, NZ)]

    mine_in = pl.ds(pl.multiple_of(par * 32, 32), 32)
    other_in = pl.ds(pl.multiple_of((1 - par) * 32, 32), 32)
    mine_out = pl.ds(pl.multiple_of(par * 16, 16), 16)
    other_out = pl.ds(pl.multiple_of((1 - par) * 16, 16), 16)
    direct, split = pl.ds(0, 3), pl.ds(3, 3)
    far = pl.ds(1, 2)

    own_frames = pltpu.make_async_copy(frames.at[0], xbuf.at[pl.ds(EDGE, ROWS)], lsem.at[0])
    own_frames.start()
    own_in, own_out = [], []
    for j in range(STRIPS):
        for side in (0, 1):
            cols = pl.ds(side * CH + j * 128, 128)
            src, dst = w_in.at[:, cols], wbuf.at[0, x, c, j, side]
            if j >= 3:
                src, dst = w_in.at[mine_in, cols], wbuf.at[0, x, c, j, side, mine_in]
            own_in.append(pltpu.make_async_copy(src, dst, lsem.at[1 + len(own_in)]))
    for side in (0, 1):
        src = w_out.at[mine_out, pl.ds(side * CH, CH)]
        own_out.append(pltpu.make_async_copy(src, vbuf.at[0, x, c, side, mine_out], lsem.at[13 + side]))
    for copy in own_in + own_out:
        copy.start()

    barrier = pltpu.get_barrier_semaphore()
    for peer in peers:
        pl.semaphore_signal(barrier, inc=1, device_id=peer, device_id_type=MESH)
    pl.semaphore_wait(barrier, len(peers))

    sent = []

    def remote(src, dst, sems, k, to):
        return pltpu.make_async_remote_copy(
            src_ref=src, dst_ref=dst, send_sem=sems[0].at[k], recv_sem=sems[1].at[k],
            device_id=to, device_id_type=MESH,
        )

    def send(*args):
        remote(*args).start()
        if args[2][0] is hsend or args[2][0] is ssend:
            sent.append(args)

    def arrived(dst, sems, k):
        remote(dst, dst, sems, k, at(dc=1)).wait_recv()

    XD = (1, 3, 2)

    def gs(j):
        return (gsend.at[j], grecv.at[j])

    qs = (qsend, qrecv)

    def z_send(j):
        src = wbuf.at[0, x, c, j, :, mine_in]
        send(src, wbuf.at[1, x, c, j, :, mine_in], gs(j), 0, at(dz=-4))
        send(src, wbuf.at[2, x, c, j, :, mine_in], gs(j), 1, at(dz=4))

    def z_wait(j):
        arrived(wbuf.at[1, x, c, j, :, mine_in], gs(j), 0)
        arrived(wbuf.at[2, x, c, j, :, mine_in], gs(j), 1)

    def x_send(j):
        ref = wbuf.at[far, x, c, j, :, mine_in]
        for i, d in enumerate(XD):
            send(ref, ref, gs(j), 2 + i, at(dx=d))

    def x_wait(j):
        for i, d in enumerate(XD):
            arrived(wbuf.at[far, (x + 4 - d) % NX, c, j, :, mine_in], gs(j), 2 + i)

    def y_send(j):
        for side, d in ((0, 1), (1, 7)):
            ref = wbuf.at[far, :, c, j, side, mine_in]
            send(ref, ref, gs(j), 5 + side, at(dy=d))

    def y_wait(j):
        for side in (0, 1):
            arrived(wbuf.at[far, :, c, j, side, other_in], gs(j), 5 + side)

    def c_send(j, part):
        ref = wbuf.at[far, :, c, j, :, (mine_in, other_in)[part]]
        send(ref, ref, gs(j), 7 + part, at(dc=1))

    def c_wait(j):
        for part in (0, 1):
            arrived(wbuf.at[far, :, 1 - c, j, :, (mine_in, other_in)[part]], gs(j), 7 + part)

    def xo_send():
        first, second = wbuf.at[0, x, c, direct], wbuf.at[0, x, c, split, :, mine_in]
        for i, d in enumerate(XD):
            send(first, first, qs, i, at(dx=d))
        for i, d in enumerate(XD):
            send(second, second, qs, 3 + i, at(dx=d))

    def xo_wait():
        for i, d in enumerate(XD):
            source = (x + 4 - d) % NX
            arrived(wbuf.at[0, source, c, direct], qs, i)
            arrived(wbuf.at[0, source, c, split, :, mine_in], qs, 3 + i)

    def own_y_send():
        for side, d in ((0, 1), (1, 7)):
            ref = wbuf.at[0, :, c, split, side, mine_in]
            send(ref, ref, qs, 6 + side, at(dy=d))

    def own_y_wait():
        for side in (0, 1):
            arrived(wbuf.at[0, :, c, split, side, other_in], qs, 6 + side)

    def own_part(part, core):
        if part == 0:
            return wbuf.at[0, :, core, direct]
        return wbuf.at[0, :, core, split, :, (mine_in, other_in)[part - 1]]

    def own_c_send(part):
        ref = own_part(part, c)
        send(ref, ref, qs, 8 + part, at(dc=1))

    def own_c_wait():
        for part in (0, 1, 2):
            arrived(own_part(part, 1 - c), qs, 8 + part)

    vs = (vsend, vrecv)

    def v_start():
        src = vbuf.at[0, x, c, :, mine_out]
        send(src, vbuf.at[1, x, c, :, mine_out], vs, 0, at(dz=-4))
        send(src, vbuf.at[2, x, c, :, mine_out], vs, 1, at(dz=4))
        for i, d in enumerate(XD):
            send(src, src, vs, 2 + i, at(dx=d))

    def v_x_send():
        arrived(vbuf.at[1, x, c, :, mine_out], vs, 0)
        arrived(vbuf.at[2, x, c, :, mine_out], vs, 1)
        ref = vbuf.at[far, x, c, :, mine_out]
        for i, d in enumerate(XD):
            send(ref, ref, vs, 5 + i, at(dx=d))

    def v_y_send():
        for i, d in enumerate(XD):
            source = (x + 4 - d) % NX
            arrived(vbuf.at[0, source, c, :, mine_out], vs, 2 + i)
            arrived(vbuf.at[far, source, c, :, mine_out], vs, 5 + i)
        for side, d in ((0, 1), (1, 7)):
            ref = vbuf.at[:, :, c, side, mine_out]
            send(ref, ref, vs, 8 + side, at(dy=d))
        ref = vbuf.at[:, :, c, :, mine_out]
        send(ref, ref, vs, 10, at(dc=1))

    def v_c_send():
        for side in (0, 1):
            arrived(vbuf.at[:, :, c, side, other_out], vs, 8 + side)
        ref = vbuf.at[:, :, c, :, other_out]
        send(ref, ref, vs, 11, at(dc=1))

    def v_wait():
        arrived(vbuf.at[:, :, 1 - c, :, mine_out], vs, 10)
        arrived(vbuf.at[:, :, 1 - c, :, other_out], vs, 11)

    for copy in own_in + own_out:
        copy.wait()
    for j in range(AHEAD):
        z_send(j)
    xo_send()
    hs = (hsend, hrecv)
    send(frames.at[0, pl.ds(ROWS - EDGE, EDGE)], xbuf.at[pl.ds(0, EDGE)], hs, 0, right)
    send(frames.at[0, pl.ds(0, EDGE)], xbuf.at[pl.ds(EDGE + ROWS, EDGE)], hs, 1, left)

    def norm(start, size):
        values = xbuf[pl.ds(start, size), :].astype(F32)
        centre = jnp.mean(values, axis=-1, keepdims=True)
        deviate = values - centre
        spread = jnp.mean(deviate * deviate, axis=-1, keepdims=True)
        normed = (deviate * lax.rsqrt(spread + 1e-05) * ln_gain[...].reshape(1, D)).astype(BF16)
        for g in range(3):
            nbuf[g, pl.ds(start, size), :] = normed[:, g * 512:(g + 1) * 512]

    own_frames.wait()

    def norm_step(i, carry):
        norm(pl.multiple_of(EDGE + i * 32, 16), 32)
        return carry

    lax.fori_loop(0, ROWS // 32, norm_step, 0)
    arrived(xbuf.at[pl.ds(0, EDGE)], hs, 0)
    norm(0, EDGE)
    arrived(xbuf.at[pl.ds(EDGE + ROWS, EDGE)], hs, 1)
    norm(EDGE + ROWS, EDGE)

    def dot(g, j, m, size):
        w = [wbuf[g, :, :, j, side].reshape(512, 128) for side in (0, 1)]
        rows = nbuf[(zh + g) % 3, pl.ds(m, size), :]
        return jnp.dot(rows, jnp.concatenate(w, axis=1), preferred_element_type=F32)

    length = lengths[0]
    HM = ALL // 2

    def gate_step(j):
        def half(m, carry):
            m0 = pl.multiple_of(m * HM, 16)
            position = t * ROWS - EDGE + m0 + lax.broadcasted_iota(jnp.int32, (HM, 128), 0)
            valid = (position >= 0) & (position < length)
            pair = dot(0, j, m0, HM) + dot(1, j, m0, HM) + dot(2, j, m0, HM)
            gated = jnp.where(valid, pair[:, :128] * sigmoid(pair[:, 128:]), 0.0)
            gbuf[j, pl.ds(m0, HM), :] = gated.astype(BF16).astype(F32)
            return carry

        lax.fori_loop(0, 2, half, 0)

    local = jnp.clip(length - t * ROWS, 0, ROWS).astype(F32)
    BLOCK = 64

    def conv_step(s):
        lanes = pl.ds(pl.multiple_of(s * 128, 128), 128)
        total = jnp.zeros((8, 128), F32)
        for b in range(0, ROWS, BLOCK):
            value = jnp.zeros((BLOCK, 128), F32)
            for k in range(TAPS):
                value = value + gbuf[s, pl.ds(b + 1 + k, BLOCK), :] * dw[pl.ds(k, 1), lanes]
            cbuf[s, pl.ds(b, BLOCK), :] = value
            position = t * ROWS + b + lax.broadcasted_iota(jnp.int32, (BLOCK, 128), 0)
            masked = jnp.where(position < length, value, 0.0)
            total = total + masked.reshape(BLOCK // 8, 8, 128).sum(axis=0)
        mean = total.sum(axis=0, keepdims=True) / jnp.maximum(local, 1.0)
        square = jnp.zeros((8, 128), F32)
        for b in range(0, ROWS, BLOCK):
            position = t * ROWS + b + lax.broadcasted_iota(jnp.int32, (BLOCK, 128), 0)
            delta = jnp.where(position < length, cbuf[s, pl.ds(b, BLOCK), :] - mean, 0.0)
            square = square + (delta * delta).reshape(BLOCK // 8, 8, 128).sum(axis=0)
        pay[s // 3, pl.ds(s % 3, 1), :] = mean
        pay[s // 3, pl.ds(s % 3 + 4, 1), :] = square.sum(axis=0, keepdims=True)
        pltpu.make_async_copy(cbuf.at[s], conv.at[s], csem.at[s]).start()

    pay[...] = jnp.zeros((2, 8, 128), F32)
    for side in (0, 1):
        pay[side, 3:4, :] = jnp.full((1, 128), local, F32)

    X_LAG, Y_LAG, C_LAG = 3, 6, 7

    def pipeline(i, carry):
        @pl.when(i < STRIPS)
        def _():
            z_wait(i)
            x_send(i)

        @pl.when(i < STRIPS - AHEAD)
        def _():
            z_send(jnp.minimum(i + AHEAD, STRIPS - 1))

        @pl.when((i >= X_LAG) & (i < STRIPS + X_LAG))
        def _():
            x_wait(i - X_LAG)
            y_send(i - X_LAG)
            c_send(i - X_LAG, 0)

        @pl.when(i == 2)
        def _():
            xo_wait()
            own_y_send()
            own_c_send(0)
            own_c_send(1)

        @pl.when(i == 4)
        def _():
            v_start()

        @pl.when(i == 6)
        def _():
            own_y_wait()
            own_c_send(2)

        @pl.when((i >= Y_LAG) & (i < STRIPS + Y_LAG))
        def _():
            y_wait(i - Y_LAG)
            c_send(i - Y_LAG, 1)

        @pl.when(i == 7)
        def _():
            own_c_wait()

        @pl.when(i == 8)
        def _():
            v_x_send()

        @pl.when(i >= C_LAG)
        def _():
            j = i - C_LAG
            c_wait(j)
            gate_step(j)
            conv_step(j)

        return carry

    lax.fori_loop(0, STRIPS + C_LAG, pipeline, 0)
    v_y_send()

    def drain(j, carry):
        src = wbuf.at[0, x, c, j, :, mine_in]
        for k in (0, 1):
            remote(src, src, gs(j), k, at(dc=1)).wait_send()
        for k in (2, 3, 4):
            ref = wbuf.at[far, x, c, j, :, mine_in]
            remote(ref, ref, gs(j), k, at(dc=1)).wait_send()
        for side in (0, 1):
            ref = wbuf.at[far, :, c, j, side, mine_in]
            remote(ref, ref, gs(j), 5 + side, at(dc=1)).wait_send()
        for part in (0, 1):
            ref = wbuf.at[far, :, c, j, :, (mine_in, other_in)[part]]
            remote(ref, ref, gs(j), 7 + part, at(dc=1)).wait_send()
        return carry

    leaving = [(wbuf.at[0, x, c, direct], qs, k) for k in (0, 1, 2)]
    leaving += [(wbuf.at[0, x, c, split, :, mine_in], qs, k) for k in (3, 4, 5)]
    leaving += [(wbuf.at[0, :, c, split, side, mine_in], qs, 6 + side) for side in (0, 1)]
    leaving += [(own_part(part, c), qs, 8 + part) for part in (0, 1, 2)]
    later = [(vbuf.at[0, x, c, :, mine_out], vs, k) for k in range(5)]
    later += [(vbuf.at[far, x, c, :, mine_out], vs, k) for k in (5, 6, 7)]
    later += [(vbuf.at[:, :, c, side, mine_out], vs, 8 + side) for side in (0, 1)]
    later += [(vbuf.at[:, :, c, :, rows], vs, 10 + k) for k, rows in enumerate((mine_out, other_out))]

    def settle(items):
        for ref, sems, k in items:
            remote(ref, ref, sems, k, at(dc=1)).wait_send()

    def after_z():
        v_c_send()
        lax.fori_loop(0, STRIPS, drain, 0)
        settle(leaving)

    wide_copies = [
        pltpu.make_async_copy(vbuf.at[g], wide.at[(zh + g) % 3], csem.at[STRIPS + g]) for g in range(3)
    ]

    def after_y():
        v_wait()
        for copy in wide_copies:
            copy.start()
        settle(later)

    def exchange(ref, slot, count, base, to, source=None, between=None):
        sems = (ssend, srecv)
        for d in range(1, count):
            src = ref.at[slot] if source is None else source(d)
            send(src, ref.at[slot], sems, base + d, to(d))
        if between is not None:
            between()
        for d in range(1, count):
            arrived(ref.at[(slot + count - d) % count], sems, base + d)
        return combine(ref, count)

    r1[slot1] = pay[c]
    r2[z] = exchange(r1, slot1, 8, 0, peer1, lambda d: pay.at[(slot1 + d) % 2])
    r3[y] = exchange(r2, z, NZ, 8, lambda d: at(dz=d), None, after_z)
    final[c] = exchange(r3, y, NY, 20, lambda d: at(dy=d), None, after_y)
    send(final.at[c], final.at[c], (ssend, srecv), 0, at(dc=1))
    for args in sent[:-1]:
        remote(*args).wait_send()
    for s in range(STRIPS):
        pltpu.make_async_copy(cbuf.at[s], conv.at[s], csem.at[s]).wait()
    for copy in wide_copies:
        copy.wait()
    arrived(final.at[1 - c], (ssend, srecv), 0)
    stats[...] = final[...]
    remote(*sent[-1]).wait_send()


TM = 256


def finish(lengths, stats, bn_gain, bn_shift, conv, wide, out, act):
    t, i = lax.axis_index("ctx"), pl.program_id(0)
    for s in range(STRIPS):
        lanes = slice(s * 128, (s + 1) * 128)
        side, row = s // 3, s % 3
        count = stats[side, 3:4, :]
        spread = stats[side, 4 + row:5 + row, :] / count
        factor = lax.rsqrt(spread + 1e-05) * bn_gain[lanes].reshape(1, 128)
        value = (conv[s] - stats[side, row:row + 1, :]) * factor + bn_shift[lanes].reshape(1, 128)
        act[:, lanes] = (value * sigmoid(value)).astype(BF16)
    start = t * ROWS + i * TM
    valid = start + lax.broadcasted_iota(jnp.int32, (TM, CH), 0) < lengths[0]
    for side in (0, 1):
        w = wide[:, :, :, side].reshape(CH, CH)
        res = jnp.dot(act[...], w, preferred_element_type=F32)
        out[0, :, side * CH:(side + 1) * CH] = jnp.where(valid, res, 0.0).astype(BF16)


def body(frames, lengths, ln_gain, w_in, dw_kernel, bn_gain, bn_shift, w_out):
    hbm = pl.BlockSpec(memory_space=pltpu.HBM)
    vmem = pl.BlockSpec(memory_space=pltpu.VMEM)
    smem = pl.BlockSpec(memory_space=pltpu.SMEM)
    wide_shape = (3, NX, 2, 2, 32, CH)
    conv, wide, stats = pl.pallas_call(
        kernel,
        out_shape=(
            jax.ShapeDtypeStruct((STRIPS, ROWS, 128), F32),
            jax.ShapeDtypeStruct(wide_shape, BF16),
            jax.ShapeDtypeStruct((2, 8, 128), F32),
        ),
        in_specs=[hbm, smem, vmem, hbm, vmem, hbm],
        out_specs=(hbm, hbm, vmem),
        scratch_shapes=[
            pltpu.VMEM((ALL, D), BF16),
            pltpu.VMEM((3, ALL, 512), BF16),
            pltpu.VMEM((3, NX, 2, STRIPS, 2, 64, 128), BF16),
            pltpu.VMEM((3, NX, 2, 2, 32, CH), BF16),
            pltpu.VMEM((STRIPS, ALL, 128), F32),
            pltpu.VMEM((STRIPS, ROWS, 128), F32),
            pltpu.VMEM((2, 8, 128), F32),
            pltpu.VMEM((8, 8, 128), F32),
            pltpu.VMEM((NZ, 8, 128), F32),
            pltpu.VMEM((NY, 8, 128), F32),
            pltpu.VMEM((2, 8, 128), F32),
            pltpu.SemaphoreType.DMA((STRIPS, 9)),
            pltpu.SemaphoreType.DMA((STRIPS, 9)),
            pltpu.SemaphoreType.DMA((11,)),
            pltpu.SemaphoreType.DMA((11,)),
            pltpu.SemaphoreType.DMA((12,)),
            pltpu.SemaphoreType.DMA((12,)),
            pltpu.SemaphoreType.DMA((2,)),
            pltpu.SemaphoreType.DMA((2,)),
            pltpu.SemaphoreType.DMA((28,)),
            pltpu.SemaphoreType.DMA((28,)),
            pltpu.SemaphoreType.DMA((15,)),
            pltpu.SemaphoreType.DMA((STRIPS + 3,)),
        ],
        compiler_params=pltpu.CompilerParams(
            collective_id=0, has_side_effects=True, vmem_limit_bytes=63 << 20
        ),
        name="conformer_conv",
    )(frames, lengths, ln_gain, w_in, dw_kernel, w_out)
    return pl.pallas_call(
        finish,
        out_shape=jax.ShapeDtypeStruct((1, ROWS, D), BF16),
        grid=(ROWS // TM,),
        in_specs=[
            smem, vmem, vmem, vmem,
            pl.BlockSpec((STRIPS, TM, 128), lambda i: (0, i, 0)),
            pl.BlockSpec(wide_shape, lambda i: (0,) * 6, pipeline_mode=pl.Buffered(1)),
        ],
        out_specs=pl.BlockSpec((1, TM, D), lambda i: (0, i, 0)),
        scratch_shapes=[pltpu.VMEM((TM, CH), BF16)],
        compiler_params=pltpu.CompilerParams(vmem_limit_bytes=63 << 20),
        name="finish",
    )(lengths, stats, bn_gain, bn_shift, conv, wide)


def solution(mesh):
    return jax.shard_map(
        body,
        mesh=mesh,
        in_specs=(
            P("fsdp", "ctx", None),
            P("fsdp"),
            P(),
            P("fsdp", None),
            P(),
            P(),
            P(),
            P("fsdp", None),
        ),
        out_specs=P("fsdp", "ctx", None),
        check_vma=False,
    )
```
